128 devices in a mesh: sub: 32 (over z, x, y_hi), node: 4 (over y_lo, core).
Axes of the slice: x: 4, y: 4 (y_hi: 2, y_lo: 2; y = y_hi * 2 + y_lo), z: 4, core: 2. Of those that a mesh axis runs over, the one named last changes fastest.
Arguments:
- search_vectors: float32 [32768, 256], P('sub'), may hold values from -60 to 60
- ritz_values: float32 [256], replicated, may hold values from -0.9 to 0.9
- matrix_blocks: float32 [256, 4, 128, 128], P('sub'), may hold values from -0.25 to 0.25
- block_lists: int32 [256, 4], P('sub'), may hold values from 0 to 255, as said below
- inverses: float32 [8, 2, 256, 128, 128], P('node', None, 'sub'), may hold values from -0.5 to 0.5
- panels: float32 [32, 512, 1024], P('sub'), may hold values from -0.1875 to 0.1875
- separator_map: int32 [32, 4], P('sub'), may hold values from 0 to 7, as said below
- separator_shift: float32 [1024], replicated, may hold values from -0.9 to 0.9
Outputs:
- normalized_vectors: float32 [32768, 256], P('sub', 'node')
The draws below stay inside these ranges and needn't reach their ends.
Inputs may be any that keep to these rules, and one draw needn't show every extreme that they name: `block_lists`: entry 0 of row g is g; the other entries of row g are distinct blocks from g - 4 to g + 4, none equal to g. `separator_map`: the entries of one row are distinct.
All inputs are finite; a program needn't handle non-finite values.
Results may differ from the reference program's by a relative error of at most 0.0001.
Values sent between devices are 32-bit elements; how exact they have to be, the bound alone decides.
No kernel may reach another device: no remote copies, remote signals or barrier semaphores. Data moves between devices by JAX's collectives and lax.ppermute only.
A program may use at most 64 MiB of HBM per device.

```python
import math
import jax
import jax.numpy as jnp
from jax import lax

VECS = 256
BLK = 128
ROWS = 1024
DEGREE = 4
HALO_BLOCKS = 4
SEP = 512
SEP_GROUPS = 8
NODES = 8
SUBS = 32
NROWS = 32768
NBLK = 8
BLOCKS = 256
SEP_BLOCKS = 4
GSEP = 1024


def draw_search_vectors(key, part):
    positions = jnp.arange(NROWS, dtype=jnp.float32) / max(NROWS - 1, 1)
    row_scale = jnp.exp(jnp.log(3.0) * positions)[:, None]
    values = jax.random.normal(jax.random.fold_in(key, 24), (NROWS, VECS), jnp.float32) * row_scale
    return jnp.clip(values, -60.0, 60.0)


def draw_block_lists(key, part):
    random_bits = jax.random.randint(jax.random.fold_in(key, 31), (BLOCKS, 2 * HALO_BLOCKS), 0, 2 ** 20, dtype=jnp.int32)
    offsets = jnp.concatenate([jnp.arange(-HALO_BLOCKS, 0, dtype=jnp.int32), jnp.arange(1, HALO_BLOCKS + 1, dtype=jnp.int32)])
    own_block = jnp.arange(BLOCKS, dtype=jnp.int32)[:, None]
    targets = own_block + offsets[None, :]
    valid = ((targets >= 0) & (targets < BLOCKS)).astype(jnp.int32)
    scores = random_bits * (2 * HALO_BLOCKS) + jnp.arange(2 * HALO_BLOCKS, dtype=jnp.int32)[None, :] + valid * 2 ** 26
    chosen_idx = lax.top_k(scores, DEGREE - 1)[1]
    chosen = jnp.take_along_axis(targets, chosen_idx, axis=1)
    return jnp.concatenate([own_block, chosen], axis=1).astype(jnp.int32)


def draw_separator_map(key, part):
    random_bits = jax.random.randint(jax.random.fold_in(key, 41), (SUBS, SEP_GROUPS), 0, 2 ** 20, dtype=jnp.int32)
    scores = random_bits * SEP_GROUPS + jnp.arange(SEP_GROUPS, dtype=jnp.int32)[None, :]
    return lax.top_k(scores, SEP_BLOCKS)[1].astype(jnp.int32)


def levels(stream_key, shape, pieces, least, largest):
    loudness = 1.0
    for position, shards_of in pieces:
        steps = jax.random.uniform(jax.random.fold_in(jax.random.fold_in(stream_key, 6), position), (shards_of,), jnp.float32, least / len(pieces), largest / len(pieces))
        loudness = loudness * jnp.repeat(jnp.exp(steps), shape[position] // shards_of).reshape((-1,) + (1,) * (len(shape) - 1 - position))
    return loudness


def noise(rng, dims, width, reach, cuts=(), kind=jnp.bfloat16):
    array = jax.random.normal(rng, dims, jnp.float32) * width
    if len(cuts) > 0:
        array = levels(rng, dims, cuts, -0.22, 0.18) * array
    return jnp.clip(array, min=-reach, max=reach).astype(kind)


def setup_inputs(seed: int = 0) -> dict:
    splits = jax.random.split(jax.random.key(seed), 9)
    search_vectors = draw_search_vectors(jax.random.fold_in(splits[8], 71), 0)
    ritz_values = jnp.clip(jax.random.uniform(splits[1], (VECS,), jnp.float32, -0.9, 0.9), -0.9, 0.9)
    matrix_blocks = noise(splits[2], (BLOCKS, DEGREE, BLK, BLK), (DEGREE * BLK) ** -0.5, 0.25, ((0, 32),), jnp.float32)
    block_lists = draw_block_lists(jax.random.fold_in(splits[8], 71), 0)
    inverses = noise(splits[4], (NODES, 2, BLOCKS, BLK, BLK), BLK ** -0.5, 0.5, ((0, 4), (2, 32)), jnp.float32)
    panels = noise(splits[5], (SUBS, SEP, ROWS), ROWS ** -0.5, 0.1875, ((0, 32),), jnp.float32)
    separator_map = draw_separator_map(jax.random.fold_in(splits[8], 71), 0)
    separator_shift = jnp.clip(jax.random.uniform(splits[7], (GSEP,), jnp.float32, -0.9, 0.9), -0.9, 0.9)
    return dict(search_vectors=search_vectors, ritz_values=ritz_values, matrix_blocks=matrix_blocks, block_lists=block_lists, inverses=inverses, panels=panels, separator_map=separator_map, separator_shift=separator_shift)


HIGHEST = lax.Precision.HIGHEST

def reference(search_vectors, ritz_values, matrix_blocks, block_lists, inverses, panels, separator_map, separator_shift):
    by_block = search_vectors.reshape(BLOCKS, BLK, VECS)

    def local_rows(operands):
        matrices, listed = operands
        return jnp.einsum('bkij,bkjm->bim', matrices, by_block[listed], precision=HIGHEST)
    product = lax.map(local_rows, (matrix_blocks.reshape(SUBS, NBLK, DEGREE, BLK, BLK), block_lists.reshape(SUBS, NBLK, DEGREE)))
    residual = product.reshape(NROWS, VECS) - search_vectors * ritz_values[None, :]
    res_blocks = residual.reshape(BLOCKS, BLK, VECS)
    one_hot = (separator_map[:, :, None] == jnp.arange(SEP_GROUPS, dtype=jnp.int32)[None, None, :]).astype(jnp.float32)
    weighted = jnp.zeros((NROWS, VECS), jnp.float32)
    for node_number in range(NODES):
        angle = math.pi * (node_number + 0.5) / NODES
        real_shift = math.cos(angle)
        imag_shift = math.sin(angle)
        first_guess = jnp.einsum('cbij,bjm->cbim', inverses[node_number], res_blocks, precision=HIGHEST)
        first_guess = first_guess.reshape(2, SUBS, ROWS, VECS)
        partial_value = jnp.einsum('tsr,ctrm->ctsm', panels, first_guess, precision=HIGHEST).reshape(2, SUBS, SEP_BLOCKS, BLK, VECS)
        separator = jnp.einsum('tpg,ctpkm->cgkm', one_hot, partial_value, precision=HIGHEST).reshape(2, GSEP, VECS)
        real_gap = (real_shift - separator_shift)[:, None]
        modulus = real_gap * real_gap + imag_shift * imag_shift
        real_part = separator[0]
        imag_part = separator[1]
        coarse = jnp.stack([(real_part * real_gap + imag_part * imag_shift) / modulus, (imag_part * real_gap - real_part * imag_shift) / modulus]).reshape(2, SEP_GROUPS, BLK, VECS)
        picked = jnp.einsum('tpg,cgkm->ctpkm', one_hot, coarse, precision=HIGHEST).reshape(2, SUBS, SEP, VECS)
        correction = jnp.einsum('tsr,ctsm->ctrm', panels, picked, precision=HIGHEST).reshape(2, BLOCKS, BLK, VECS)
        products = jnp.einsum('cbij,dbjm->cdbim', inverses[node_number], correction, precision=HIGHEST).reshape(2, 2, NROWS, VECS)
        first_flat = first_guess.reshape(2, NROWS, VECS)
        sol_real = first_flat[0] - (products[0, 0] - products[1, 1])
        sol_imag = first_flat[1] - (products[0, 1] + products[1, 0])
        weight_real = 2.0 * real_shift / NODES
        weight_imag = 2.0 * imag_shift / NODES
        weighted = weighted + weight_real * sol_real - weight_imag * sol_imag
    update = search_vectors - weighted
    factor = lax.rsqrt(lax.optimization_barrier(jnp.mean(update * update, axis=0)) + 1e-06)
    return update * factor[None, :]
```

```python
import functools
import math

import jax
import jax.numpy as jnp
import numpy as np
from jax import lax
from jax.experimental import pallas as pl
from jax.experimental.pallas import tpu as pltpu
from jax.sharding import PartitionSpec as P

BLK = 128
HALO = 4
GROUPS = 8
NODES = 8
LOCAL = 2
LANES = 128

F32 = jnp.float32
BF16 = jnp.bfloat16
VMEM = pl.BlockSpec(memory_space=pltpu.VMEM)
SMEM = pl.BlockSpec(memory_space=pltpu.SMEM)


def split(x):
    hi = x.astype(BF16)
    return hi, (x - hi.astype(F32)).astype(BF16)


def dot(a, b, dims=((1,), (0,))):
    return lax.dot_general(a, b, (dims, ((), ())), preferred_element_type=F32)


def dot3(a, b, dims=((1,), (0,))):
    return dot(a[0], b[0], dims) + (dot(a[0], b[1], dims) + dot(a[1], b[0], dims))


def halves(top, bottom):
    low = lax.broadcasted_iota(jnp.int32, top.shape, 1) < LANES // 2
    return (
        jnp.where(low, top, pltpu.roll(bottom, LANES // 2, 1)),
        jnp.where(low, pltpu.roll(top, LANES // 2, 1), bottom),
    )


def forward_kernel(
    place, lists, sep_map, own, near, far, ritz, mats, inverses, panel,
    residual, pieces, ext_hi, ext_lo, guess_hi, guess_lo,
):
    sub, core = place[0], place[1] % 2
    blocks = own.shape[0] // BLK
    for ref, start in ((near, core * 12), (own, HALO), (far, 12 - core * 12)):
        hi, lo = split(ref[...].reshape(-1, BLK, ref.shape[1]))
        ext_hi[pl.ds(start, hi.shape[0])] = hi
        ext_lo[pl.ds(start, hi.shape[0])] = lo
    for g in range(blocks):
        where = [lists[g, q] - sub * blocks + HALO for q in range(4)]
        rhs = [jnp.concatenate([e[w] for w in where], 0) for e in (ext_hi, ext_lo)]
        lhs = split(jnp.concatenate([mats[g, q] for q in range(4)], 1))
        rows = slice(g * BLK, (g + 1) * BLK)
        res = dot3(lhs, rhs) - own[rows, :] * ritz[...]
        residual[rows, :] = res
        r_hi, r_lo = split(res)
        d_hi, d_lo = split(
            jnp.concatenate([inverses[n, c, g] for n in range(LOCAL) for c in range(2)], 0)
        )
        guess = dot(
            jnp.concatenate([d_hi, d_lo, d_hi], 1), jnp.concatenate([r_hi, r_hi, r_lo], 0)
        )
        for k in range(2 * LOCAL):
            hi, lo = split(guess[k * BLK : (k + 1) * BLK])
            guess_hi[rows, k * 256 : (k + 1) * 256] = hi
            guess_lo[rows, k * 256 : (k + 1) * 256] = lo
    p_hi, p_lo = split(panel[0])
    for k in range(2 * LOCAL):
        cols = slice(k * 256, (k + 1) * 256)
        part = dot3((p_hi, p_lo), (guess_hi[:, cols], guess_lo[:, cols]))
        n, c = divmod(k, 2)
        for p in range(4):
            for h in range(2):
                row = ((c * 4 + p) * 2 + h) * 8
                tile = part[p * BLK : (p + 1) * BLK, h * LANES : (h + 1) * LANES]
                pieces[n * 16 : (n + 1) * 16, row : row + 8, :] = tile.reshape(16, 8, LANES)
    lane = lax.broadcasted_iota(jnp.int32, (8, LANES), 1)
    ids = jnp.zeros((8, LANES), jnp.int32)
    for p in range(4):
        ids = jnp.where(lane == p, sep_map[0, p], ids)
    pieces[:, 128:136, :] = jnp.broadcast_to(ids.astype(F32)[None], (32, 8, LANES))


def owner_kernel(place, maps, table, shift, received, back, total):
    sub = place[0]
    node = place[1] * LOCAL + sub // 16
    first_row = (sub % 16) * 8
    z_r, z_i, w_r, w_i = (table[node, k] for k in range(4))
    total[...] = jnp.zeros_like(total)

    def add(t, carry):
        for p in range(4):
            g = maps[t, p]
            for c in range(2):
                r = (c * 4 + p) * 16
                total[g, c] += received[t, r : r + 16, :]
        return carry

    lax.fori_loop(0, 32, add, 0, unroll=4)
    lane = lax.broadcasted_iota(jnp.int32, (8, LANES), 1)
    pick = lane == first_row + lax.broadcasted_iota(jnp.int32, (8, LANES), 0)
    for g in range(GROUPS):
        row = jnp.broadcast_to(shift[g : g + 1, :], (8, LANES))
        gap = z_r - jnp.sum(jnp.where(pick, row, 0.0), axis=1, keepdims=True)
        gap = jnp.concatenate([gap, gap], 0)
        modulus = gap * gap + z_i * z_i
        real, imag = total[g, 0], total[g, 1]
        c_r = (real * gap + imag * z_i) / modulus
        c_i = (imag * gap - real * z_i) / modulus
        total[g, 0] = w_r * c_r - w_i * c_i
        total[g, 1] = w_r * c_i + w_i * c_r

    def give(t, carry):
        for p in range(4):
            g = maps[t, p]
            for c in range(2):
                r = (c * 4 + p) * 16
                back[t, r : r + 16, :] = total[g, c]
        return carry

    lax.fori_loop(0, 32, give, 0, unroll=4)


def backward_kernel(
    place, table, picked, residual, inverses, panel, keep, send, x_hi, x_lo, v_hi, v_lo
):
    core = place[1] % 2
    for n in range(LOCAL):
        for c in range(2):
            for p in range(4):
                for h in range(2):
                    row = ((c * 4 + p) * 2 + h) * 8
                    tile = picked[n * 16 : (n + 1) * 16, row : row + 8, :].reshape(BLK, LANES)
                    hi, lo = split(tile)
                    col = (n * 2 + c) * 256 + h * LANES
                    x_hi[p * BLK : (p + 1) * BLK, col : col + LANES] = hi
                    x_lo[p * BLK : (p + 1) * BLK, col : col + LANES] = lo
    panels = split(panel[0])
    res = residual[...]
    blocks = residual.shape[0] // BLK
    for n in range(LOCAL):
        for c in range(2):
            k = n * 2 + c
            cols = slice(k * 256, (k + 1) * 256)
            corr = dot3(panels, (x_hi[:, cols], x_lo[:, cols]), ((0,), (0,)))
            weight = table[place[1] * LOCAL + n, 2 + c]
            value = res * weight - corr
            hi, lo = split(value if c == 0 else -value)
            v_hi[:, k] = hi.reshape(blocks, BLK, 256)
            v_lo[:, k] = lo.reshape(blocks, BLK, 256)
    for g in range(blocks):
        lhs = split(
            jnp.concatenate([inverses[n, c, g] for n in range(LOCAL) for c in range(2)], 1)
        )
        rhs = v_hi[g].reshape(4 * BLK, 256), v_lo[g].reshape(4 * BLK, 256)
        weighted = dot3(lhs, rhs)
        low, high = halves(weighted[:, :LANES], weighted[:, LANES:])
        rows = slice(g * BLK, (g + 1) * BLK)
        keep[rows, :] = jnp.where(core == 0, low, high)
        send[rows, :] = jnp.where(core == 0, high, low)


def pair_kernel(place, mine, theirs, keep, send):
    first = place[1] // 2 == 0
    half = mine.shape[0] // 2
    total = mine[...] + theirs[...]
    low, high = halves(total[:half], total[half:])
    keep[...] = jnp.where(first, low, high)
    send[...] = jnp.where(first, high, low)


def update_kernel(place, mine, theirs, vectors, update, squares):
    first, core = place[1] // 2 == 0, place[1] % 2
    half = mine.shape[0]
    mid = vectors.shape[1] // 2
    own = jnp.where(first, vectors[:, :mid], vectors[:, mid:])
    low, high = halves(own[:half], own[half:])
    new = jnp.where(core == 0, low, high) - (mine[...] + theirs[...])
    update[...] = new
    sums = jnp.sum(new * new, axis=0, keepdims=True)
    sums = sums + pltpu.roll(sums, LANES // 2, 1)
    squares[...] = jnp.broadcast_to(sums[None], squares.shape)


def scale_kernel(rows, update, squares, out):
    half = update.shape[0]
    factor = lax.rsqrt(jnp.sum(squares[...], axis=0) / rows + 1e-06)
    new = update[...] * factor
    out[:half, :] = new[:, : LANES // 2]
    out[half:, :] = pltpu.roll(new, LANES // 2, 1)[:, : LANES // 2]


def call(body, name, specs, shapes, scratch=()):
    return pl.pallas_call(
        body,
        name=name,
        in_specs=specs,
        out_specs=[VMEM] * len(shapes),
        out_shape=[jax.ShapeDtypeStruct(s, F32) for s in shapes],
        scratch_shapes=list(scratch),
        compiler_params=pltpu.CompilerParams(vmem_limit_bytes=50 << 20),
    )


def shards(
    search_vectors,
    ritz_values,
    matrix_blocks,
    block_lists,
    inverses,
    panels,
    separator_map,
    separator_shift,
):
    rows, width = search_vectors.shape
    subs, nodes = lax.axis_size("sub"), lax.axis_size("node")
    sub, node = lax.axis_index("sub"), lax.axis_index("node")
    place = jnp.stack([sub, node]).astype(jnp.int32)
    theta = math.pi * (np.arange(NODES) + 0.5) / NODES
    z = np.stack([np.cos(theta), np.sin(theta)], 1)
    table = jnp.asarray(np.concatenate([z, 2.0 * z / NODES], 1), F32)

    halo_rows = HALO * BLK
    edge = lax.dynamic_slice_in_dim(
        search_vectors, jnp.where(node % 2 == 0, rows - halo_rows, 0), halo_rows, 0
    )
    ring = []
    for t in range(subs):
        for n in range(nodes):
            d = t + 1 if n % 2 == 0 else t - 1
            if 0 <= d < subs:
                ring.append((t * nodes + n, d * nodes + n))
    swap_core = [(i, i ^ 1) for i in range(nodes)]
    swap_chip = [(i, i ^ 2) for i in range(nodes)]
    near = lax.ppermute(edge, ("sub", "node"), ring)
    far = lax.ppermute(near, "node", swap_core)

    residual, pieces = call(
        forward_kernel,
        "forward",
        [SMEM, SMEM, SMEM] + [VMEM] * 7,
        [(rows, width), (subs, 136, LANES)],
        [
            pltpu.VMEM((16, BLK, width), BF16),
            pltpu.VMEM((16, BLK, width), BF16),
            pltpu.VMEM((rows, 4 * width), BF16),
            pltpu.VMEM((rows, 4 * width), BF16),
        ],
    )(
        place, block_lists, separator_map, search_vectors, near, far,
        ritz_values[None, :], matrix_blocks, inverses, panels,
    )
    received = lax.all_to_all(pieces, "sub", 0, 0, tiled=True)
    maps = received[:, 128, :4].astype(jnp.int32)
    (back,) = call(
        owner_kernel,
        "owner",
        [SMEM, SMEM, SMEM, VMEM, VMEM],
        [(subs, 128, LANES)],
        [pltpu.VMEM((GROUPS, 2, 16, LANES), F32)],
    )(place, maps, table, separator_shift.reshape(GROUPS, LANES), received)
    picked = lax.all_to_all(back, "sub", 0, 0, tiled=True)
    keep, send = call(
        backward_kernel,
        "backward",
        [SMEM, SMEM] + [VMEM] * 4,
        [(rows, LANES), (rows, LANES)],
        [
            pltpu.VMEM((512, 4 * width), BF16),
            pltpu.VMEM((512, 4 * width), BF16),
            pltpu.VMEM((rows // BLK, 4, BLK, width), BF16),
            pltpu.VMEM((rows // BLK, 4, BLK, width), BF16),
        ],
    )(place, table, picked, residual, inverses, panels)
    theirs = lax.ppermute(send, "node", swap_core)
    keep, send = call(
        pair_kernel, "pair", [SMEM, VMEM, VMEM], [(rows // 2, LANES), (rows // 2, LANES)]
    )(place, keep, theirs)
    theirs = lax.ppermute(send, "node", swap_chip)
    update, squares = call(
        update_kernel,
        "update",
        [SMEM, VMEM, VMEM, VMEM],
        [(rows // 2, LANES), (subs, 1, LANES)],
    )(place, keep, theirs, search_vectors)
    gathered = lax.all_to_all(squares, "sub", 0, 0, tiled=True)
    (out,) = call(
        functools.partial(scale_kernel, rows * subs),
        "scale",
        [VMEM, VMEM],
        [(rows, width // nodes)],
    )(update, gathered)
    return out


def solution(mesh):
    return jax.shard_map(
        shards,
        mesh=mesh,
        in_specs=(
            P("sub", None),
            P(),
            P("sub", None, None, None),
            P("sub", None),
            P("node", None, "sub", None, None),
            P("sub", None, None),
            P("sub", None),
            P(),
        ),
        out_specs=P("sub", "node"),
        check_vma=False,
    )
```

```python
import functools
import math

import jax
import jax.numpy as jnp
import numpy as np
from jax import lax
from jax.experimental import pallas as pl
from jax.experimental.pallas import tpu as pltpu
from jax.sharding import PartitionSpec as P

BLK = 128
HALO = 4
GROUPS = 8
NODES = 8
LOCAL = 2
LANES = 128

F32 = jnp.float32
BF16 = jnp.bfloat16
VMEM = pl.BlockSpec(memory_space=pltpu.VMEM)
SMEM = pl.BlockSpec(memory_space=pltpu.SMEM)


def split(x):
    hi = x.astype(BF16)
    return hi, (x - hi.astype(F32)).astype(BF16)


def dot(a, b, dims=((1,), (0,))):
    return lax.dot_general(a, b, (dims, ((), ())), preferred_element_type=F32)


def dot3(a, b, dims=((1,), (0,))):
    return dot(a[0], b[0], dims) + (dot(a[0], b[1], dims) + dot(a[1], b[0], dims))


def halves(top, bottom):
    low = lax.broadcasted_iota(jnp.int32, top.shape, 1) < LANES // 2
    return (
        jnp.where(low, top, pltpu.roll(bottom, LANES // 2, 1)),
        jnp.where(low, pltpu.roll(top, LANES // 2, 1), bottom),
    )


def prepare_kernel(
    place, sep_map, table, own, ritz, mats, inverses, panel,
    own_hi, own_lo, scaled, m_hi, m_lo, e_hi, e_lo, f_hi, f_lo, w_hi, w_lo, ids,
):
    node = place[1] * LOCAL
    blocks, sep = own.shape[0] // BLK, panel.shape[1]
    scaled[...] = own[...] * ritz[...]
    parts = [(n, c) for n in range(LOCAL) for c in range(2)]
    for g in range(blocks):
        rows = slice(g * BLK, (g + 1) * BLK)
        own_hi[g], own_lo[g] = split(own[rows, :])
        m_hi[g], m_lo[g] = split(jnp.concatenate([mats[g, q] for q in range(4)], 1))
        weighted = [inverses[n, 0, g] * table[node + n, 2] for n in range(LOCAL)]
        weighted += [inverses[n, 1, g] * -table[node + n, 3] for n in range(LOCAL)]
        w_hi[g], w_lo[g] = split(sum(weighted[1:], weighted[0]))
        p_hi, p_lo = split(panel[0, :, rows])
        d_hi, d_lo = split(jnp.concatenate([inverses[n, c, g] for n, c in parts], 1))
        e = dot(
            jnp.concatenate([p_hi, p_lo, p_hi], 1), jnp.concatenate([d_hi, d_hi, d_lo], 0)
        )
        d_hi, d_lo = split(
            jnp.concatenate([-inverses[n, c, g] if c == 0 else inverses[n, c, g] for n, c in parts], 0)
        )
        f = dot(
            jnp.concatenate([d_hi, d_lo, d_hi], 1),
            jnp.concatenate([p_hi, p_hi, p_lo], 1),
            ((1,), (1,)),
        )
        for k in range(2 * LOCAL):
            span, block = slice(k * sep, (k + 1) * sep), slice(k * BLK, (k + 1) * BLK)
            e_hi[span, rows], e_lo[span, rows] = split(e[:, block])
            f_hi[rows, span], f_lo[rows, span] = split(f[block, :])
    lane = lax.broadcasted_iota(jnp.int32, ids.shape, 1)
    value = jnp.zeros(ids.shape, jnp.int32)
    for p in range(4):
        value = jnp.where(lane == p, sep_map[0, p], value)
    ids[...] = value.astype(F32)


def forward_kernel(
    place, lists, near, far, own_hi, own_lo, scaled, m_hi, m_lo, e_hi, e_lo, ids,
    r_hi, r_lo, pieces, ext_hi, ext_lo,
):
    sub, core = place[0], place[1] % 2
    blocks = own_hi.shape[0]
    for ref, start in ((near, core * 12), (far, 12 - core * 12)):
        hi, lo = split(ref[...].reshape(HALO, BLK, ref.shape[1]))
        ext_hi[pl.ds(start, HALO)] = hi
        ext_lo[pl.ds(start, HALO)] = lo
    ext_hi[HALO : HALO + blocks] = own_hi[...]
    ext_lo[HALO : HALO + blocks] = own_lo[...]
    for g in range(blocks):
        where = [lists[q, g] - sub * blocks + HALO for q in range(4)]
        rhs = [jnp.concatenate([e[w] for w in where], 0) for e in (ext_hi, ext_lo)]
        rows = slice(g * BLK, (g + 1) * BLK)
        r_hi[rows, :], r_lo[rows, :] = split(dot3((m_hi[g], m_lo[g]), rhs) - scaled[rows, :])
    sep = e_hi.shape[0] // (2 * LOCAL)
    res = r_hi[...], r_lo[...]
    for k in range(2 * LOCAL):
        span = slice(k * sep, (k + 1) * sep)
        part = dot3((e_hi[span, :], e_lo[span, :]), res)
        n, c = divmod(k, 2)
        for p in range(4):
            for h in range(2):
                row = ((c * 4 + p) * 2 + h) * 8
                tile = part[p * BLK : (p + 1) * BLK, h * LANES : (h + 1) * LANES]
                pieces[n * 16 : (n + 1) * 16, row : row + 8, :] = tile.reshape(16, 8, LANES)
    pieces[:, 128:136, :] = jnp.broadcast_to(ids[...][None], (32, 8, LANES))


def owner_kernel(place, maps, table, shift, received, back, total):
    sub = place[0]
    node = place[1] * LOCAL + sub // 16
    first_row = (sub % 16) * 8
    z_r, z_i, w_r, w_i = (table[node, k] for k in range(4))
    total[...] = jnp.zeros_like(total)

    def add(t, carry):
        for p in range(4):
            g = maps[t, p]
            for c in range(2):
                r = (c * 4 + p) * 16
                total[g, c] += received[t, r : r + 16, :]
        return carry

    lax.fori_loop(0, 32, add, 0, unroll=4)
    lane = lax.broadcasted_iota(jnp.int32, (8, LANES), 1)
    pick = lane == first_row + lax.broadcasted_iota(jnp.int32, (8, LANES), 0)
    for g in range(GROUPS):
        row = jnp.broadcast_to(shift[g : g + 1, :], (8, LANES))
        gap = z_r - jnp.sum(jnp.where(pick, row, 0.0), axis=1, keepdims=True)
        gap = jnp.concatenate([gap, gap], 0)
        modulus = gap * gap + z_i * z_i
        real, imag = total[g, 0], total[g, 1]
        c_r = (real * gap + imag * z_i) / modulus
        c_i = (imag * gap - real * z_i) / modulus
        total[g, 0] = w_r * c_r - w_i * c_i
        total[g, 1] = w_r * c_i + w_i * c_r

    def give(t, carry):
        for p in range(4):
            g = maps[t, p]
            for c in range(2):
                r = (c * 4 + p) * 16
                back[t, r : r + 16, :] = total[g, c]
        return carry

    lax.fori_loop(0, 32, give, 0, unroll=4)


def backward_kernel(
    place, picked, f_hi, f_lo, r_hi, r_lo, w_hi, w_lo, keep, send, x_hi, x_lo
):
    core = place[1] % 2
    sep = f_hi.shape[1] // (2 * LOCAL)
    for k in range(2 * LOCAL):
        n, c = divmod(k, 2)
        for p in range(4):
            for h in range(2):
                row = ((c * 4 + p) * 2 + h) * 8
                tile = picked[n * 16 : (n + 1) * 16, row : row + 8, :].reshape(BLK, LANES)
                rows = slice(k * sep + p * BLK, k * sep + (p + 1) * BLK)
                cols = slice(h * LANES, (h + 1) * LANES)
                x_hi[rows, cols], x_lo[rows, cols] = split(tile)
    coarse = x_hi[...], x_lo[...]
    for g in range(0, w_hi.shape[0], 2):
        both = slice(g * BLK, (g + 2) * BLK)
        back = dot3((f_hi[both, :], f_lo[both, :]), coarse)
        for i in range(2):
            rows = slice((g + i) * BLK, (g + i + 1) * BLK)
            weighted = back[i * BLK : (i + 1) * BLK] + dot3(
                (w_hi[g + i], w_lo[g + i]), (r_hi[rows, :], r_lo[rows, :])
            )
            low, high = halves(weighted[:, :LANES], weighted[:, LANES:])
            keep[rows, :] = jnp.where(core == 0, low, high)
            send[rows, :] = jnp.where(core == 0, high, low)


def pair_kernel(place, mine, theirs, keep, send):
    first = place[1] // 2 == 0
    half = mine.shape[0] // 2
    total = mine[...] + theirs[...]
    low, high = halves(total[:half], total[half:])
    keep[...] = jnp.where(first, low, high)
    send[...] = jnp.where(first, high, low)


def update_kernel(place, mine, theirs, vectors, update, squares):
    first, core = place[1] // 2 == 0, place[1] % 2
    half = mine.shape[0]
    mid = vectors.shape[1] // 2
    own = jnp.where(first, vectors[:, :mid], vectors[:, mid:])
    low, high = halves(own[:half], own[half:])
    new = jnp.where(core == 0, low, high) - (mine[...] + theirs[...])
    update[...] = new
    sums = jnp.sum(new * new, axis=0, keepdims=True)
    sums = sums + pltpu.roll(sums, LANES // 2, 1)
    squares[...] = jnp.broadcast_to(sums[None], squares.shape)


def scale_kernel(rows, update, squares, out):
    half = update.shape[0]
    factor = lax.rsqrt(jnp.sum(squares[...], axis=0) / rows + 1e-06)
    new = (update[...] * factor).T
    out[:, :half] = new[: LANES // 2]
    out[:, half:] = new[LANES // 2 :]


def call(body, name, specs, shapes, scratch=(), limit=16, flops=0):
    shapes = [s if isinstance(s, jax.ShapeDtypeStruct) else jax.ShapeDtypeStruct(s, F32) for s in shapes]
    return pl.pallas_call(
        body,
        name=name,
        in_specs=specs,
        out_specs=[VMEM] * len(shapes),
        out_shape=shapes,
        scratch_shapes=list(scratch),
        cost_estimate=pl.CostEstimate(flops=flops, bytes_accessed=8 << 20, transcendentals=0),
        compiler_params=pltpu.CompilerParams(vmem_limit_bytes=limit << 20),
    )


def shards(
    search_vectors,
    ritz_values,
    matrix_blocks,
    block_lists,
    inverses,
    panels,
    separator_map,
    separator_shift,
):
    rows, width = search_vectors.shape
    subs, nodes = lax.axis_size("sub"), lax.axis_size("node")
    sub, node = lax.axis_index("sub"), lax.axis_index("node")
    place = jnp.stack([sub, node]).astype(jnp.int32)
    theta = math.pi * (np.arange(NODES) + 0.5) / NODES
    z = np.stack([np.cos(theta), np.sin(theta)], 1)
    table = jnp.asarray(np.concatenate([z, 2.0 * z / NODES], 1), F32)

    halo_rows = HALO * BLK
    edge = lax.dynamic_slice_in_dim(
        search_vectors, jnp.where(node % 2 == 0, rows - halo_rows, 0), halo_rows, 0
    )
    ring = []
    for t in range(subs):
        for n in range(nodes):
            d = t + 1 if n % 2 == 0 else t - 1
            if 0 <= d < subs:
                ring.append((t * nodes + n, d * nodes + n))
    swap_core = [(i, i ^ 1) for i in range(nodes)]
    swap_chip = [(i, i ^ 2) for i in range(nodes)]
    near = lax.ppermute(edge, ("sub", "node"), ring)
    half = functools.partial(jax.ShapeDtypeStruct, dtype=BF16)
    blocks, sep = rows // BLK, panels.shape[1]
    prepared = call(
        prepare_kernel,
        "prepare",
        [SMEM, SMEM, SMEM] + [VMEM] * 5,
        [half((blocks, BLK, width))] * 2
        + [(rows, width)]
        + [half((blocks, BLK, 4 * BLK))] * 2
        + [half((4 * sep, rows))] * 2
        + [half((rows, 4 * sep))] * 2
        + [half((blocks, BLK, BLK))] * 2
        + [(8, LANES)],
        limit=24,
        flops=8 * 10**9,
    )(
        place, separator_map, table, search_vectors, ritz_values[None, :],
        matrix_blocks, inverses, panels,
    )
    own_hi, own_lo, scaled, m_hi, m_lo, e_hi, e_lo, f_hi, f_lo, w_hi, w_lo, ids = prepared
    near, ids = lax.optimization_barrier((near, ids))
    far = lax.ppermute(near, "node", swap_core)
    r_hi, r_lo, pieces = call(
        forward_kernel,
        "forward",
        [SMEM, SMEM] + [VMEM] * 10,
        [half((rows, width)), half((rows, width)), (subs, 136, LANES)],
        [pltpu.VMEM((16, BLK, width), BF16)] * 2,
        limit=16,
        flops=4 * 10**9,
    )(
        place, block_lists.T, near, far, own_hi, own_lo, scaled, m_hi, m_lo, e_hi, e_lo, ids
    )
    received = lax.all_to_all(pieces, "sub", 0, 0, tiled=True)
    maps = received[:, 128, :4].astype(jnp.int32)
    (back,) = call(
        owner_kernel,
        "owner",
        [SMEM, SMEM, SMEM, VMEM, VMEM],
        [(subs, 128, LANES)],
        [pltpu.VMEM((GROUPS, 2, 16, LANES), F32)],
    )(place, maps, table, separator_shift.reshape(GROUPS, LANES), received)
    picked = lax.all_to_all(back, "sub", 0, 0, tiled=True)
    keep, send = call(
        backward_kernel,
        "backward",
        [SMEM] + [VMEM] * 7,
        [(rows, LANES), (rows, LANES)],
        [pltpu.VMEM((4 * sep, width), BF16)] * 2,
        limit=16,
        flops=4 * 10**9,
    )(place, picked, f_hi, f_lo, r_hi, r_lo, w_hi, w_lo)
    theirs = lax.ppermute(send, "node", swap_core)
    keep, send = call(
        pair_kernel, "pair", [SMEM, VMEM, VMEM], [(rows // 2, LANES), (rows // 2, LANES)]
    )(place, keep, theirs)
    theirs = lax.ppermute(send, "node", swap_chip)
    update, squares = call(
        update_kernel,
        "update",
        [SMEM, VMEM, VMEM, VMEM],
        [(rows // 2, LANES), (subs, 1, LANES)],
    )(place, keep, theirs, search_vectors)
    gathered = lax.all_to_all(squares, "sub", 0, 0, tiled=True)
    (out,) = call(
        functools.partial(scale_kernel, rows * subs),
        "scale",
        [VMEM, VMEM],
        [(width // nodes, rows)],
    )(update, gathered)
    return out.T


def solution(mesh):
    return jax.shard_map(
        shards,
        mesh=mesh,
        in_specs=(
            P("sub", None),
            P(),
            P("sub", None, None, None),
            P("sub", None),
            P("node", None, "sub", None, None),
            P("sub", None, None),
            P("sub", None),
            P(),
        ),
        out_specs=P("sub", "node"),
        check_vma=False,
    )
```

```python
import functools
import math

import jax
import jax.numpy as jnp
from jax import lax
from jax.experimental import pallas as pl
from jax.experimental.pallas import tpu as pltpu
from jax.sharding import PartitionSpec as P

BLK = 128
HALO = 4
GROUPS = 8
NODES = 8
LOCAL = 2
LANES = 128

F32 = jnp.float32
BF16 = jnp.bfloat16
VMEM = pl.BlockSpec(memory_space=pltpu.VMEM)
SMEM = pl.BlockSpec(memory_space=pltpu.SMEM)
HBM = pl.BlockSpec(memory_space=pltpu.HBM)

THETA = [math.pi * (j + 0.5) / NODES for j in range(NODES)]
Z_REAL, Z_IMAG = [math.cos(t) for t in THETA], [math.sin(t) for t in THETA]
W_REAL, W_IMAG = [2.0 * v / NODES for v in Z_REAL], [2.0 * v / NODES for v in Z_IMAG]


def split(x):
    hi = x.astype(BF16)
    return hi, (x - hi.astype(F32)).astype(BF16)


def dot(a, b, dims=((1,), (0,))):
    return lax.dot_general(a, b, (dims, ((), ())), preferred_element_type=F32)


def dot3(a, b, dims=((1,), (0,))):
    return dot(a[0], b[0], dims) + (dot(a[0], b[1], dims) + dot(a[1], b[0], dims))


def halves(top, bottom):
    low = lax.broadcasted_iota(jnp.int32, top.shape, 1) < LANES // 2
    return (
        jnp.where(low, top, pltpu.roll(bottom, LANES // 2, 1)),
        jnp.where(low, pltpu.roll(top, LANES // 2, 1), bottom),
    )


def constant(node, values):
    out = jnp.float32(values[0])
    for k in range(1, NODES):
        out = jnp.where(node == k, jnp.float32(values[k]), out)
    return out


def prepare_kernel(
    place, sep_map, own_hbm, ritz_hbm, mats_hbm, inverses_hbm, panel_hbm,
    own_hi, own_lo, scaled, m_hi, m_lo, e_hi, e_lo, f_hi, f_lo, w_hi, w_lo, ids,
    own, ritz, mats, inverses, panel, ids_sem, ritz_sem, sems, map_copy,
):
    node = place[1] * LOCAL
    blocks, sep = own.shape[0] // BLK, panel.shape[0]
    parts = [(n, c) for n in range(LOCAL) for c in range(2)]
    copies = []
    for g in range(blocks):
        rows = pl.ds(g * BLK, BLK)
        copies.append(
            [
                pltpu.make_async_copy(src, dst, sems.at[g, k])
                for k, (src, dst) in enumerate(
                    (
                        (panel_hbm.at[0, :, rows], panel.at[:, rows]),
                        (inverses_hbm.at[:, :, g], inverses.at[g]),
                        (mats_hbm.at[g], mats.at[g]),
                        (own_hbm.at[rows, :], own.at[rows, :]),
                    )
                )
            ]
        )
    small = [
        pltpu.make_async_copy(ritz_hbm, ritz, ritz_sem),
        pltpu.make_async_copy(sep_map, map_copy, ids_sem),
    ]
    for copy in copies[0] + small + sum(copies[1:], []):
        copy.start()
    for copy in small:
        copy.wait()
    for g in range(blocks):
        for copy in copies[g]:
            copy.wait()
        rows = slice(g * BLK, (g + 1) * BLK)
        scaled[rows, :] = own[rows, :] * ritz[...]
        own_hi[g], own_lo[g] = split(own[rows, :])
        m_hi[g], m_lo[g] = split(jnp.concatenate([mats[g, q] for q in range(4)], 1))
        weighted = []
        for n in range(LOCAL):
            weighted.append(inverses[g, n, 0] * constant(node + n, W_REAL))
            weighted.append(inverses[g, n, 1] * -constant(node + n, W_IMAG))
        w_hi[g], w_lo[g] = split(sum(weighted[1:], weighted[0]))
        p_hi, p_lo = split(panel[:, rows])
        d_hi, d_lo = split(jnp.concatenate([inverses[g, n, c] for n, c in parts], 1))
        e = dot(
            jnp.concatenate([p_hi, p_lo, p_hi], 1), jnp.concatenate([d_hi, d_hi, d_lo], 0)
        )
        d_hi, d_lo = split(
            jnp.concatenate([-inverses[g, n, c] if c == 0 else inverses[g, n, c] for n, c in parts], 0)
        )
        f = dot(
            jnp.concatenate([d_hi, d_lo, d_hi], 1),
            jnp.concatenate([p_hi, p_hi, p_lo], 1),
            ((1,), (1,)),
        )
        for k in range(2 * LOCAL):
            span, block = slice(k * sep, (k + 1) * sep), slice(k * BLK, (k + 1) * BLK)
            e_hi[span, rows], e_lo[span, rows] = split(e[:, block])
            f_hi[rows, span], f_lo[rows, span] = split(f[block, :])
    lane = lax.broadcasted_iota(jnp.int32, ids.shape, 1)
    value = jnp.zeros(ids.shape, jnp.int32)
    for p in range(4):
        value = jnp.where(lane == p, map_copy[0, p], value)
    ids[...] = value.astype(F32)


def forward_kernel(
    place, lists, near, far, own_hi, own_lo, scaled, m_hi, m_lo, e_hi, e_lo, ids,
    r_hi, r_lo, pieces, ext_hi, ext_lo,
):
    sub, core = place[0], place[1] % 2
    blocks = own_hi.shape[0]
    for ref, start in ((near, core * 12), (far, 12 - core * 12)):
        hi, lo = split(ref[...].reshape(HALO, BLK, ref.shape[1]))
        ext_hi[pl.ds(start, HALO)] = hi
        ext_lo[pl.ds(start, HALO)] = lo
    ext_hi[HALO : HALO + blocks] = own_hi[...]
    ext_lo[HALO : HALO + blocks] = own_lo[...]
    for g in range(blocks):
        where = [lists[q, g] - sub * blocks + HALO for q in range(4)]
        rhs = [jnp.concatenate([e[w] for w in where], 0) for e in (ext_hi, ext_lo)]
        rows = slice(g * BLK, (g + 1) * BLK)
        r_hi[rows, :], r_lo[rows, :] = split(dot3((m_hi[g], m_lo[g]), rhs) - scaled[rows, :])
    sep = e_hi.shape[0] // (2 * LOCAL)
    res = r_hi[...], r_lo[...]
    for k in range(2 * LOCAL):
        span = slice(k * sep, (k + 1) * sep)
        part = dot3((e_hi[span, :], e_lo[span, :]), res)
        n, c = divmod(k, 2)
        for p in range(4):
            for h in range(2):
                row = ((c * 4 + p) * 2 + h) * 8
                tile = part[p * BLK : (p + 1) * BLK, h * LANES : (h + 1) * LANES]
                pieces[n * 16 : (n + 1) * 16, row : row + 8, :] = tile.reshape(16, 8, LANES)
    pieces[:, 128:136, :] = jnp.broadcast_to(ids[...][None], (32, 8, LANES))


def owner_kernel(place, maps, shift, received, back, total):
    sub = place[0]
    node = place[1] * LOCAL + sub // 16
    first_row = (sub % 16) * 8
    z_r, z_i, w_r, w_i = (constant(node, v) for v in (Z_REAL, Z_IMAG, W_REAL, W_IMAG))
    total[...] = jnp.zeros_like(total)

    def add(t, carry):
        for p in range(4):
            g = maps[t, p]
            for c in range(2):
                r = (c * 4 + p) * 16
                total[g, c] += received[t, r : r + 16, :]
        return carry

    lax.fori_loop(0, 32, add, 0, unroll=4)
    lane = lax.broadcasted_iota(jnp.int32, (8, LANES), 1)
    pick = lane == first_row + lax.broadcasted_iota(jnp.int32, (8, LANES), 0)
    for g in range(GROUPS):
        row = jnp.broadcast_to(shift[g : g + 1, :], (8, LANES))
        gap = z_r - jnp.sum(jnp.where(pick, row, 0.0), axis=1, keepdims=True)
        gap = jnp.concatenate([gap, gap], 0)
        modulus = gap * gap + z_i * z_i
        real, imag = total[g, 0], total[g, 1]
        c_r = (real * gap + imag * z_i) / modulus
        c_i = (imag * gap - real * z_i) / modulus
        total[g, 0] = w_r * c_r - w_i * c_i
        total[g, 1] = w_r * c_i + w_i * c_r

    def give(t, carry):
        for p in range(4):
            g = maps[t, p]
            for c in range(2):
                r = (c * 4 + p) * 16
                back[t, r : r + 16, :] = total[g, c]
        return carry

    lax.fori_loop(0, 32, give, 0, unroll=4)


def backward_kernel(
    place, picked, f_hi, f_lo, r_hi, r_lo, w_hi, w_lo, keep, send, x_hi, x_lo
):
    core = place[1] % 2
    sep = f_hi.shape[1] // (2 * LOCAL)
    for k in range(2 * LOCAL):
        n, c = divmod(k, 2)
        for p in range(4):
            for h in range(2):
                row = ((c * 4 + p) * 2 + h) * 8
                tile = picked[n * 16 : (n + 1) * 16, row : row + 8, :].reshape(BLK, LANES)
                rows = slice(k * sep + p * BLK, k * sep + (p + 1) * BLK)
                cols = slice(h * LANES, (h + 1) * LANES)
                x_hi[rows, cols], x_lo[rows, cols] = split(tile)
    coarse = x_hi[...], x_lo[...]
    for g in range(0, w_hi.shape[0], 2):
        both = slice(g * BLK, (g + 2) * BLK)
        back = dot3((f_hi[both, :], f_lo[both, :]), coarse)
        for i in range(2):
            rows = slice((g + i) * BLK, (g + i + 1) * BLK)
            weighted = back[i * BLK : (i + 1) * BLK] + dot3(
                (w_hi[g + i], w_lo[g + i]), (r_hi[rows, :], r_lo[rows, :])
            )
            low, high = halves(weighted[:, :LANES], weighted[:, LANES:])
            keep[rows, :] = jnp.where(core == 0, low, high)
            send[rows, :] = jnp.where(core == 0, high, low)


def pair_kernel(place, mine, theirs, keep, send):
    first = place[1] // 2 == 0
    half = mine.shape[0] // 2
    total = mine[...] + theirs[...]
    low, high = halves(total[:half], total[half:])
    keep[...] = jnp.where(first, low, high)
    send[...] = jnp.where(first, high, low)


def update_kernel(place, mine, theirs, vectors, update, squares):
    first, core = place[1] // 2 == 0, place[1] % 2
    half = mine.shape[0]
    mid = vectors.shape[1] // 2
    own = jnp.where(first, vectors[:, :mid], vectors[:, mid:])
    low, high = halves(own[:half], own[half:])
    new = jnp.where(core == 0, low, high) - (mine[...] + theirs[...])
    update[...] = new
    sums = jnp.sum(new * new, axis=0, keepdims=True)
    sums = sums + pltpu.roll(sums, LANES // 2, 1)
    squares[...] = jnp.broadcast_to(sums[None], squares.shape)


def scale_kernel(rows, update, squares, out):
    half = update.shape[0]
    factor = lax.rsqrt(jnp.sum(squares[...], axis=0) / rows + 1e-06)
    new = (update[...] * factor).T
    out[:, :half] = new[: LANES // 2]
    out[:, half:] = new[LANES // 2 :]


def call(body, name, specs, shapes, scratch=(), limit=16, flops=0):
    shapes = [s if isinstance(s, jax.ShapeDtypeStruct) else jax.ShapeDtypeStruct(s, F32) for s in shapes]
    return pl.pallas_call(
        body,
        name=name,
        in_specs=specs,
        out_specs=[VMEM] * len(shapes),
        out_shape=shapes,
        scratch_shapes=list(scratch),
        cost_estimate=pl.CostEstimate(flops=flops, bytes_accessed=8 << 20, transcendentals=0),
        compiler_params=pltpu.CompilerParams(vmem_limit_bytes=limit << 20),
    )


def shards(
    search_vectors,
    ritz_values,
    matrix_blocks,
    block_lists,
    inverses,
    panels,
    separator_map,
    separator_shift,
):
    rows, width = search_vectors.shape
    subs, nodes = lax.axis_size("sub"), lax.axis_size("node")
    sub, node = lax.axis_index("sub"), lax.axis_index("node")
    place = jnp.stack([sub, node]).astype(jnp.int32)

    halo_rows = HALO * BLK
    edge = lax.dynamic_slice_in_dim(
        search_vectors, jnp.where(node % 2 == 0, rows - halo_rows, 0), halo_rows, 0
    )
    ring = []
    for t in range(subs):
        for n in range(nodes):
            d = t + 1 if n % 2 == 0 else t - 1
            if 0 <= d < subs:
                ring.append((t * nodes + n, d * nodes + n))
    swap_core = [(i, i ^ 1) for i in range(nodes)]
    swap_chip = [(i, i ^ 2) for i in range(nodes)]
    near = lax.ppermute(edge, ("sub", "node"), ring)
    half = functools.partial(jax.ShapeDtypeStruct, dtype=BF16)
    blocks, sep = rows // BLK, panels.shape[1]
    prepared = call(
        prepare_kernel,
        "prepare",
        [SMEM] + [HBM] * 6,
        [half((blocks, BLK, width))] * 2
        + [(rows, width)]
        + [half((blocks, BLK, 4 * BLK))] * 2
        + [half((4 * sep, rows))] * 2
        + [half((rows, 4 * sep))] * 2
        + [half((blocks, BLK, BLK))] * 2
        + [(8, LANES)],
        [
            pltpu.VMEM((rows, width), F32),
            pltpu.VMEM((1, width), F32),
            pltpu.VMEM(matrix_blocks.shape, F32),
            pltpu.VMEM((blocks, LOCAL, 2, BLK, BLK), F32),
            pltpu.VMEM((sep, rows), F32),
            pltpu.SemaphoreType.DMA,
            pltpu.SemaphoreType.DMA,
            pltpu.SemaphoreType.DMA((blocks, 4)),
            pltpu.SMEM(separator_map.shape, jnp.int32),
        ],
        limit=24,
        flops=8 * 10**9,
    )(
        place, *(
            pltpu.with_memory_space_constraint(x, pltpu.HBM)
            for x in (
                separator_map, search_vectors, ritz_values[None, :],
                matrix_blocks, inverses, panels,
            )
        )
    )
    own_hi, own_lo, scaled, m_hi, m_lo, e_hi, e_lo, f_hi, f_lo, w_hi, w_lo, ids = prepared
    near, ids = lax.optimization_barrier((near, ids))
    far = lax.ppermute(near, "node", swap_core)
    r_hi, r_lo, pieces = call(
        forward_kernel,
        "forward",
        [SMEM, SMEM] + [VMEM] * 10,
        [half((rows, width)), half((rows, width)), (subs, 136, LANES)],
        [pltpu.VMEM((16, BLK, width), BF16)] * 2,
        limit=16,
        flops=4 * 10**9,
    )(
        place, block_lists.T, near, far, own_hi, own_lo, scaled, m_hi, m_lo, e_hi, e_lo, ids
    )
    received = lax.all_to_all(pieces, "sub", 0, 0, tiled=True)
    maps = received[:, 128, :4].astype(jnp.int32)
    (back,) = call(
        owner_kernel,
        "owner",
        [SMEM, SMEM, VMEM, VMEM],
        [(subs, 128, LANES)],
        [pltpu.VMEM((GROUPS, 2, 16, LANES), F32)],
    )(place, maps, separator_shift.reshape(GROUPS, LANES), received)
    picked = lax.all_to_all(back, "sub", 0, 0, tiled=True)
    keep, send = call(
        backward_kernel,
        "backward",
        [SMEM] + [VMEM] * 7,
        [(rows, LANES), (rows, LANES)],
        [pltpu.VMEM((4 * sep, width), BF16)] * 2,
        limit=16,
        flops=4 * 10**9,
    )(place, picked, f_hi, f_lo, r_hi, r_lo, w_hi, w_lo)
    theirs = lax.ppermute(send, "node", swap_core)
    keep, send = call(
        pair_kernel, "pair", [SMEM, VMEM, VMEM], [(rows // 2, LANES), (rows // 2, LANES)]
    )(place, keep, theirs)
    theirs = lax.ppermute(send, "node", swap_chip)
    update, squares = call(
        update_kernel,
        "update",
        [SMEM, VMEM, VMEM, VMEM],
        [(rows // 2, LANES), (subs, 1, LANES)],
    )(place, keep, theirs, search_vectors)
    gathered = lax.all_to_all(squares, "sub", 0, 0, tiled=True)
    (out,) = call(
        functools.partial(scale_kernel, rows * subs),
        "scale",
        [VMEM, VMEM],
        [(width // nodes, rows)],
    )(update, gathered)
    return out.T


def solution(mesh):
    return jax.shard_map(
        shards,
        mesh=mesh,
        in_specs=(
            P("sub", None),
            P(),
            P("sub", None, None, None),
            P("sub", None),
            P("node", None, "sub", None, None),
            P("sub", None, None),
            P("sub", None),
            P(),
        ),
        out_specs=P("sub", "node"),
        check_vma=False,
    )
```

```python
import functools
import math

import jax
import jax.numpy as jnp
from jax import lax
from jax.experimental import pallas as pl
from jax.experimental.pallas import tpu as pltpu
from jax.sharding import PartitionSpec as P

BLK = 128
HALO = 4
GROUPS = 8
NODES = 8
LOCAL = 2
LANES = 128

F32 = jnp.float32
BF16 = jnp.bfloat16
VMEM = pl.BlockSpec(memory_space=pltpu.VMEM)
SMEM = pl.BlockSpec(memory_space=pltpu.SMEM)
HBM = pl.BlockSpec(memory_space=pltpu.HBM)

THETA = [math.pi * (j + 0.5) / NODES for j in range(NODES)]
Z_REAL, Z_IMAG = [math.cos(t) for t in THETA], [math.sin(t) for t in THETA]
W_REAL, W_IMAG = [2.0 * v / NODES for v in Z_REAL], [2.0 * v / NODES for v in Z_IMAG]


def split(x):
    hi = x.astype(BF16)
    return hi, (x - hi.astype(F32)).astype(BF16)


def dot(a, b, dims=((1,), (0,))):
    return lax.dot_general(a, b, (dims, ((), ())), preferred_element_type=F32)


def dot3(a, b, dims=((1,), (0,))):
    return dot(a[0], b[0], dims) + (dot(a[0], b[1], dims) + dot(a[1], b[0], dims))


def halves(top, bottom):
    low = lax.broadcasted_iota(jnp.int32, top.shape, 1) < LANES // 2
    return (
        jnp.where(low, top, pltpu.roll(bottom, LANES // 2, 1)),
        jnp.where(low, pltpu.roll(top, LANES // 2, 1), bottom),
    )


def constant(node, values):
    out = jnp.float32(values[0])
    for k in range(1, NODES):
        out = jnp.where(node == k, jnp.float32(values[k]), out)
    return out


def prepare_kernel(
    place, sep_map, own_hbm, ritz_hbm, mats_hbm, inverses_hbm, panel_hbm,
    own_hi, own_lo, scaled, m_hi, m_lo, e_hi, e_lo, f_hi, f_lo, w_hi, w_lo, ids,
    own, ritz, mats, inverses, panel, ids_sem, ritz_sem, mats_sem, panel_sem, sems, map_copy,
):
    node, core = place[1] * LOCAL, place[1] % 2
    blocks, sep = own.shape[0] // BLK, panel.shape[0]
    per_core = blocks // 2
    parts = [(n, c) for n in range(LOCAL) for c in range(2)]
    copies = []
    for g in range(blocks):
        rows = pl.ds(g * BLK, BLK)
        copies.append(
            (
                pltpu.make_async_copy(inverses_hbm.at[:, :, g], inverses.at[g], sems.at[g, 0]),
                pltpu.make_async_copy(own_hbm.at[rows, :], own.at[rows, :], sems.at[g, 1]),
            )
        )
    my_mats = pltpu.make_async_copy(
        mats_hbm.at[pl.ds(core * per_core, per_core)], mats, mats_sem
    )
    whole_panel = pltpu.make_async_copy(panel_hbm.at[0], panel, panel_sem)
    small = [
        pltpu.make_async_copy(ritz_hbm, ritz, ritz_sem),
        pltpu.make_async_copy(sep_map, map_copy, ids_sem),
    ]
    for copy in [whole_panel, *copies[0], *sum(copies[1:], ()), my_mats] + small:
        copy.start()
    whole_panel.wait()
    for g in range(blocks):
        for copy in copies[g]:
            copy.wait()
        rows = slice(g * BLK, (g + 1) * BLK)
        own_hi[g], own_lo[g] = split(own[rows, :])
        weighted = []
        for n in range(LOCAL):
            weighted.append(inverses[g, n, 0] * constant(node + n, W_REAL))
            weighted.append(inverses[g, n, 1] * -constant(node + n, W_IMAG))
        w_hi[g], w_lo[g] = split(sum(weighted[1:], weighted[0]))
        p_hi, p_lo = split(panel[:, rows])
        d_hi, d_lo = split(jnp.concatenate([inverses[g, n, c] for n, c in parts], 1))
        e = dot(
            jnp.concatenate([p_hi, p_lo, p_hi], 1), jnp.concatenate([d_hi, d_hi, d_lo], 0)
        )
        d_hi, d_lo = split(
            jnp.concatenate([-inverses[g, n, c] if c == 0 else inverses[g, n, c] for n, c in parts], 0)
        )
        f = dot(
            jnp.concatenate([d_hi, d_lo, d_hi], 1),
            jnp.concatenate([p_hi, p_hi, p_lo], 1),
            ((1,), (1,)),
        )
        side, first = divmod(g, per_core)
        cols = slice(first * BLK, (first + 1) * BLK)
        for k in range(2 * LOCAL):
            span, block = slice(k * sep, (k + 1) * sep), slice(k * BLK, (k + 1) * BLK)
            e_hi[side, span, cols], e_lo[side, span, cols] = split(e[:, block])
            f_hi[rows, span], f_lo[rows, span] = split(f[block, :])
    for copy in small:
        copy.wait()
    my_mats.wait()
    for g in range(per_core):
        rows = pl.ds(pl.multiple_of((core * per_core + g) * BLK, BLK), BLK)
        scaled[g] = own[rows, :] * ritz[...]
        m_hi[g], m_lo[g] = split(jnp.concatenate([mats[g, q] for q in range(4)], 1))
    lane = lax.broadcasted_iota(jnp.int32, ids.shape, 1)
    value = jnp.zeros(ids.shape, jnp.int32)
    for p in range(4):
        value = jnp.where(lane == p, map_copy[0, p], value)
    ids[...] = value.astype(F32)


def residual_kernel(
    place, lists, halo, own_hi, own_lo, scaled, m_hi, m_lo, residual, r_hi, r_lo, ext_hi, ext_lo
):
    sub, core = place[0], place[1] % 2
    blocks, per_core = own_hi.shape[0], m_hi.shape[0]
    hi, lo = split(halo[...].reshape(HALO, BLK, halo.shape[1]))
    ext_hi[pl.ds(core * blocks, HALO)] = hi
    ext_lo[pl.ds(core * blocks, HALO)] = lo
    start = HALO - core * HALO
    ext_hi[pl.ds(start, blocks)] = own_hi[...]
    ext_lo[pl.ds(start, blocks)] = own_lo[...]
    for g in range(per_core):
        where = [lists[q, core * per_core + g] - sub * blocks + start for q in range(4)]
        rhs = [jnp.concatenate([e[w] for w in where], 0) for e in (ext_hi, ext_lo)]
        rows = slice(g * BLK, (g + 1) * BLK)
        res = dot3((m_hi[g], m_lo[g]), rhs) - scaled[g]
        residual[rows, :] = res
        r_hi[rows, :], r_lo[rows, :] = split(res)


def mine_kernel(place, e_hi, e_lo, r_hi, r_lo, sums):
    core = place[1] % 2
    sums[...] = dot3((e_hi[core], e_lo[core]), (r_hi[...], r_lo[...]))


def theirs_kernel(
    place, sums, theirs, e_hi, e_lo, m_hi, m_lo, ids, r_hi, r_lo, pieces
):
    core = place[1] % 2
    other = 1 - core
    hi, lo = split(theirs[...])
    r_hi[other], r_lo[other] = hi, lo
    r_hi[core], r_lo[core] = m_hi[...], m_lo[...]
    sep = e_hi.shape[1] // (2 * LOCAL)
    for k in range(2 * LOCAL):
        span = slice(k * sep, (k + 1) * sep)
        part = sums[span, :] + dot3((e_hi[other, span, :], e_lo[other, span, :]), (hi, lo))
        n, c = divmod(k, 2)
        for p in range(4):
            for h in range(2):
                row = ((c * 4 + p) * 2 + h) * 8
                tile = part[p * BLK : (p + 1) * BLK, h * LANES : (h + 1) * LANES]
                pieces[n * 16 : (n + 1) * 16, row : row + 8, :] = tile.reshape(16, 8, LANES)
    pieces[:, 128:136, :] = jnp.broadcast_to(ids[...][None], (32, 8, LANES))


def owner_kernel(place, maps, shift, received, back, total):
    sub = place[0]
    node = place[1] * LOCAL + sub // 16
    first_row = (sub % 16) * 8
    z_r, z_i, w_r, w_i = (constant(node, v) for v in (Z_REAL, Z_IMAG, W_REAL, W_IMAG))
    total[...] = jnp.zeros_like(total)

    def add(t, carry):
        for p in range(4):
            g = maps[t, p]
            for c in range(2):
                r = (c * 4 + p) * 16
                total[g, c] += received[t, r : r + 16, :]
        return carry

    lax.fori_loop(0, 32, add, 0, unroll=4)
    lane = lax.broadcasted_iota(jnp.int32, (8, LANES), 1)
    pick = lane == first_row + lax.broadcasted_iota(jnp.int32, (8, LANES), 0)
    for g in range(GROUPS):
        row = jnp.broadcast_to(shift[g : g + 1, :], (8, LANES))
        gap = z_r - jnp.sum(jnp.where(pick, row, 0.0), axis=1, keepdims=True)
        gap = jnp.concatenate([gap, gap], 0)
        modulus = gap * gap + z_i * z_i
        real, imag = total[g, 0], total[g, 1]
        c_r = (real * gap + imag * z_i) / modulus
        c_i = (imag * gap - real * z_i) / modulus
        total[g, 0] = w_r * c_r - w_i * c_i
        total[g, 1] = w_r * c_i + w_i * c_r

    def give(t, carry):
        for p in range(4):
            g = maps[t, p]
            for c in range(2):
                r = (c * 4 + p) * 16
                back[t, r : r + 16, :] = total[g, c]
        return carry

    lax.fori_loop(0, 32, give, 0, unroll=4)


def coarse_halves(picked, x_hi, x_lo):
    sep = x_hi.shape[0] // (2 * LOCAL)
    for k in range(2 * LOCAL):
        n, c = divmod(k, 2)
        for p in range(4):
            for h in range(2):
                row = ((c * 4 + p) * 2 + h) * 8
                tile = picked[n * 16 : (n + 1) * 16, row : row + 8, :].reshape(BLK, LANES)
                rows = slice(k * sep + p * BLK, k * sep + (p + 1) * BLK)
                cols = slice(h * LANES, (h + 1) * LANES)
                x_hi[rows, cols], x_lo[rows, cols] = split(tile)


def solve(side, core, coarse, f_hi, f_lo, r_hi, r_lo, w_hi, w_lo, keep, send):
    per_side = w_hi.shape[0] // 2
    for g in range(0, per_side, 2):
        first = side * per_side + g
        both = slice(first * BLK, (first + 2) * BLK)
        back = dot3((f_hi[both, :], f_lo[both, :]), coarse)
        for i in range(2):
            rows = slice((g + i) * BLK, (g + i + 1) * BLK)
            weighted = back[i * BLK : (i + 1) * BLK] + dot3(
                (w_hi[first + i], w_lo[first + i]), (r_hi[side, rows, :], r_lo[side, rows, :])
            )
            low, high = halves(weighted[:, :LANES], weighted[:, LANES:])
            keep[rows, :] = jnp.where(core == 0, low, high)
            send[rows, :] = jnp.where(core == 0, high, low)


def first_kernel(place, picked, f_hi, f_lo, r_hi, r_lo, w_hi, w_lo, keep, send, x_hi, x_lo):
    coarse_halves(picked, x_hi, x_lo)
    coarse = x_hi[...], x_lo[...]
    solve(0, place[1] % 2, coarse, f_hi, f_lo, r_hi, r_lo, w_hi, w_lo, keep, send)


def second_kernel(place, x_hi, x_lo, f_hi, f_lo, r_hi, r_lo, w_hi, w_lo, keep, send):
    coarse = x_hi[...], x_lo[...]
    solve(1, place[1] % 2, coarse, f_hi, f_lo, r_hi, r_lo, w_hi, w_lo, keep, send)


def pair_kernel(place, mine, theirs, keep, send):
    first = place[1] // 2 == 0
    half = mine.shape[0] // 2
    total = mine[...] + theirs[...]
    low, high = halves(total[:half], total[half:])
    keep[...] = jnp.where(first, low, high)
    send[...] = jnp.where(first, high, low)


def update_kernel(place, mine_a, theirs_a, mine_b, theirs_b, vectors, update, squares):
    first, core = place[1] // 2 == 0, place[1] % 2
    quarter = mine_a.shape[0]
    mid = vectors.shape[1] // 2
    own = jnp.where(first, vectors[:, :mid], vectors[:, mid:])
    sums = jnp.zeros((1, LANES), F32)
    for side, (mine, theirs) in enumerate(((mine_a, theirs_a), (mine_b, theirs_b))):
        top = own[2 * side * quarter : (2 * side + 1) * quarter]
        low, high = halves(top, own[(2 * side + 1) * quarter : (2 * side + 2) * quarter])
        new = jnp.where(core == 0, low, high) - (mine[...] + theirs[...])
        update[side * quarter : (side + 1) * quarter, :] = new
        sums = sums + jnp.sum(new * new, axis=0, keepdims=True)
    sums = sums + pltpu.roll(sums, LANES // 2, 1)
    squares[...] = jnp.broadcast_to(sums[None], squares.shape)


def scale_kernel(rows, update, squares, out):
    quarter = update.shape[0] // 2
    factor = lax.rsqrt(jnp.sum(squares[...], axis=0) / rows + 1e-06)
    new = (update[...] * factor).T
    for side in range(2):
        for h in range(2):
            start = (2 * side + h) * quarter
            out[:, start : start + quarter] = new[
                h * (LANES // 2) : (h + 1) * (LANES // 2), side * quarter : (side + 1) * quarter
            ]


def call(body, name, specs, shapes, scratch=(), limit=16, flops=0):
    shapes = [s if isinstance(s, jax.ShapeDtypeStruct) else jax.ShapeDtypeStruct(s, F32) for s in shapes]
    return pl.pallas_call(
        body,
        name=name,
        in_specs=specs,
        out_specs=[VMEM] * len(shapes),
        out_shape=shapes,
        scratch_shapes=list(scratch),
        cost_estimate=pl.CostEstimate(flops=flops, bytes_accessed=8 << 20, transcendentals=0),
        compiler_params=pltpu.CompilerParams(vmem_limit_bytes=limit << 20),
    )


def shards(
    search_vectors,
    ritz_values,
    matrix_blocks,
    block_lists,
    inverses,
    panels,
    separator_map,
    separator_shift,
):
    rows, width = search_vectors.shape
    subs, nodes = lax.axis_size("sub"), lax.axis_size("node")
    sub, node = lax.axis_index("sub"), lax.axis_index("node")
    place = jnp.stack([sub, node]).astype(jnp.int32)

    halo_rows = HALO * BLK
    edge = lax.dynamic_slice_in_dim(
        search_vectors, jnp.where(node % 2 == 0, rows - halo_rows, 0), halo_rows, 0
    )
    ring = []
    for t in range(subs):
        for n in range(nodes):
            d = t + 1 if n % 2 == 0 else t - 1
            if 0 <= d < subs:
                ring.append((t * nodes + n, d * nodes + n))
    swap_core = [(i, i ^ 1) for i in range(nodes)]
    swap_chip = [(i, i ^ 2) for i in range(nodes)]
    halo = lax.ppermute(edge, ("sub", "node"), ring)

    half = functools.partial(jax.ShapeDtypeStruct, dtype=BF16)
    blocks, sep = rows // BLK, panels.shape[1]
    per_core = blocks // 2
    prepared = call(
        prepare_kernel,
        "prepare",
        [SMEM] + [HBM] * 6,
        [half((blocks, BLK, width))] * 2
        + [(per_core, BLK, width)]
        + [half((per_core, BLK, 4 * BLK))] * 2
        + [half((2, 4 * sep, rows // 2))] * 2
        + [half((rows, 4 * sep))] * 2
        + [half((blocks, BLK, BLK))] * 2
        + [(8, LANES)],
        [
            pltpu.VMEM((rows, width), F32),
            pltpu.VMEM((1, width), F32),
            pltpu.VMEM((per_core, 4, BLK, BLK), F32),
            pltpu.VMEM((blocks, LOCAL, 2, BLK, BLK), F32),
            pltpu.VMEM((sep, rows), F32),
            pltpu.SemaphoreType.DMA,
            pltpu.SemaphoreType.DMA,
            pltpu.SemaphoreType.DMA,
            pltpu.SemaphoreType.DMA,
            pltpu.SemaphoreType.DMA((blocks, 2)),
            pltpu.SMEM(separator_map.shape, jnp.int32),
        ],
        limit=24,
        flops=8 * 10**9,
    )(
        place, *(
            pltpu.with_memory_space_constraint(x, pltpu.HBM)
            for x in (
                separator_map, search_vectors, ritz_values[None, :],
                matrix_blocks, inverses, panels,
            )
        )
    )
    own_hi, own_lo, scaled, m_hi, m_lo, e_hi, e_lo, f_hi, f_lo, w_hi, w_lo, ids = prepared
    halo, ids = lax.optimization_barrier((halo, ids))
    residual, mine_hi, mine_lo = call(
        residual_kernel,
        "residual",
        [SMEM, SMEM] + [VMEM] * 6,
        [(rows // 2, width)] + [half((rows // 2, width))] * 2,
        [pltpu.VMEM((blocks + HALO, BLK, width), BF16)] * 2,
        flops=10**9,
    )(place, block_lists.T, halo, own_hi, own_lo, scaled, m_hi, m_lo)
    theirs = lax.ppermute(residual, "node", swap_core)
    (sums,) = call(
        mine_kernel,
        "mine",
        [SMEM] + [VMEM] * 4,
        [(4 * sep, width)],
        flops=4 * 10**9,
    )(place, e_hi, e_lo, mine_hi, mine_lo)
    theirs, sums = lax.optimization_barrier((theirs, sums))
    r_hi, r_lo, pieces = call(
        theirs_kernel,
        "theirs",
        [SMEM] + [VMEM] * 7,
        [half((2, rows // 2, width))] * 2 + [(subs, 136, LANES)],
        flops=4 * 10**9,
    )(place, sums, theirs, e_hi, e_lo, mine_hi, mine_lo, ids)
    received = lax.all_to_all(pieces, "sub", 0, 0, tiled=True)
    maps = received[:, 128, :4].astype(jnp.int32)
    (back,) = call(
        owner_kernel,
        "owner",
        [SMEM, SMEM, VMEM, VMEM],
        [(subs, 128, LANES)],
        [pltpu.VMEM((GROUPS, 2, 16, LANES), F32)],
    )(place, maps, separator_shift.reshape(GROUPS, LANES), received)
    picked = lax.all_to_all(back, "sub", 0, 0, tiled=True)
    operators = (f_hi, f_lo, r_hi, r_lo, w_hi, w_lo)
    keep_a, send_a, x_hi, x_lo = call(
        first_kernel,
        "first",
        [SMEM] + [VMEM] * 7,
        [(rows // 2, LANES)] * 2 + [half((4 * sep, width))] * 2,
        flops=2 * 10**9,
    )(place, picked, *operators)
    theirs_a = lax.ppermute(send_a, "node", swap_core)
    keep_b, send_b = call(
        second_kernel,
        "second",
        [SMEM] + [VMEM] * 8,
        [(rows // 2, LANES)] * 2,
        flops=2 * 10**9,
    )(place, x_hi, x_lo, *operators)
    theirs_a, send_b = lax.optimization_barrier((theirs_a, send_b))
    theirs_b = lax.ppermute(send_b, "node", swap_core)
    pair = call(pair_kernel, "pair", [SMEM, VMEM, VMEM], [(rows // 4, LANES)] * 2)
    keep_a, send_a = pair(place, keep_a, theirs_a)
    theirs_a = lax.ppermute(send_a, "node", swap_chip)
    keep_b, send_b = pair(place, keep_b, theirs_b)
    theirs_b = lax.ppermute(send_b, "node", swap_chip)
    update, squares = call(
        update_kernel,
        "update",
        [SMEM] + [VMEM] * 5,
        [(rows // 2, LANES), (subs, 1, LANES)],
    )(place, keep_a, theirs_a, keep_b, theirs_b, search_vectors)
    gathered = lax.all_to_all(squares, "sub", 0, 0, tiled=True)
    (out,) = call(
        functools.partial(scale_kernel, rows * subs),
        "scale",
        [VMEM, VMEM],
        [(width // nodes, rows)],
    )(update, gathered)
    return out.T


def solution(mesh):
    return jax.shard_map(
        shards,
        mesh=mesh,
        in_specs=(
            P("sub", None),
            P(),
            P("sub", None, None, None),
            P("sub", None),
            P("node", None, "sub", None, None),
            P("sub", None, None),
            P("sub", None),
            P(),
        ),
        out_specs=P("sub", "node"),
        check_vma=False,
    )
```

```python
import functools
import math

import jax
import jax.numpy as jnp
from jax import lax
from jax.experimental import pallas as pl
from jax.experimental.pallas import tpu as pltpu
from jax.sharding import PartitionSpec as P

BLK = 128
HALO = 4
GROUPS = 8
NODES = 8
LOCAL = 2
LANES = 128

F32 = jnp.float32
BF16 = jnp.bfloat16
VMEM = pl.BlockSpec(memory_space=pltpu.VMEM)
SMEM = pl.BlockSpec(memory_space=pltpu.SMEM)
HBM = pl.BlockSpec(memory_space=pltpu.HBM)

THETA = [math.pi * (j + 0.5) / NODES for j in range(NODES)]
Z_REAL, Z_IMAG = [math.cos(t) for t in THETA], [math.sin(t) for t in THETA]
W_REAL, W_IMAG = [2.0 * v / NODES for v in Z_REAL], [2.0 * v / NODES for v in Z_IMAG]


def split(x):
    hi = x.astype(BF16)
    return hi, (x - hi.astype(F32)).astype(BF16)


def dot(a, b, dims=((1,), (0,))):
    return lax.dot_general(a, b, (dims, ((), ())), preferred_element_type=F32)


def dot3(a, b, dims=((1,), (0,))):
    return dot(a[0], b[0], dims) + (dot(a[0], b[1], dims) + dot(a[1], b[0], dims))


def halves(top, bottom):
    low = lax.broadcasted_iota(jnp.int32, top.shape, 1) < LANES // 2
    return (
        jnp.where(low, top, pltpu.roll(bottom, LANES // 2, 1)),
        jnp.where(low, pltpu.roll(top, LANES // 2, 1), bottom),
    )


def constant(node, values):
    out = jnp.float32(values[0])
    for k in range(1, NODES):
        out = jnp.where(node == k, jnp.float32(values[k]), out)
    return out


def prepare_kernel(
    place, sep_map, own_hbm, ritz_hbm, mats_hbm, inverses_hbm, panel_hbm,
    own_hi, own_lo, scaled, m_hi, m_lo, e_hi, e_lo, f_hi, f_lo, w_hi, w_lo, ids, columns,
    own, ritz, mats, inverses, panel, ids_sem, ritz_sem, mats_sem, panel_sem, sems, map_copy,
):
    node, core = place[1] * LOCAL, place[1] % 2
    blocks, sep = own.shape[0] // BLK, panel.shape[0]
    per_core = blocks // 2
    parts = [(n, c) for n in range(LOCAL) for c in range(2)]
    copies = []
    for g in range(blocks):
        rows = pl.ds(g * BLK, BLK)
        copies.append(
            (
                pltpu.make_async_copy(inverses_hbm.at[:, :, g], inverses.at[g], sems.at[g, 0]),
                pltpu.make_async_copy(own_hbm.at[rows, :], own.at[rows, :], sems.at[g, 1]),
            )
        )
    my_mats = pltpu.make_async_copy(
        mats_hbm.at[pl.ds(core * per_core, per_core)], mats, mats_sem
    )
    whole_panel = pltpu.make_async_copy(panel_hbm.at[0], panel, panel_sem)
    small = [
        pltpu.make_async_copy(ritz_hbm, ritz, ritz_sem),
        pltpu.make_async_copy(sep_map, map_copy, ids_sem),
    ]
    for copy in [whole_panel, *copies[0], *sum(copies[1:], ()), my_mats] + small:
        copy.start()
    whole_panel.wait()
    for g in range(blocks):
        for copy in copies[g]:
            copy.wait()
        rows = slice(g * BLK, (g + 1) * BLK)
        own_hi[g], own_lo[g] = split(own[rows, :])
        weighted = []
        for n in range(LOCAL):
            weighted.append(inverses[g, n, 0] * constant(node + n, W_REAL))
            weighted.append(inverses[g, n, 1] * -constant(node + n, W_IMAG))
        w_hi[g], w_lo[g] = split(sum(weighted[1:], weighted[0]))
        p_hi, p_lo = split(panel[:, rows])
        d_hi, d_lo = split(jnp.concatenate([inverses[g, n, c] for n, c in parts], 1))
        e = dot(
            jnp.concatenate([p_hi, p_lo, p_hi], 1), jnp.concatenate([d_hi, d_hi, d_lo], 0)
        )
        d_hi, d_lo = split(
            jnp.concatenate([-inverses[g, n, c] if c == 0 else inverses[g, n, c] for n, c in parts], 0)
        )
        f = dot(
            jnp.concatenate([d_hi, d_lo, d_hi], 1),
            jnp.concatenate([p_hi, p_hi, p_lo], 1),
            ((1,), (1,)),
        )
        side, nth = divmod(g, per_core)
        cols = slice(nth * BLK, (nth + 1) * BLK)
        for k in range(2 * LOCAL):
            span, block = slice(k * sep, (k + 1) * sep), slice(k * BLK, (k + 1) * BLK)
            e_hi[side, span, cols], e_lo[side, span, cols] = split(e[:, block])
            f_hi[rows, span], f_lo[rows, span] = split(f[block, :])
    for copy in small:
        copy.wait()
    my_mats.wait()
    first, mid, quarter = place[1] // 2 == 0, own.shape[1] // 2, own.shape[0] // 4
    for side in range(2):
        top, bottom = (
            jnp.where(first, own[rows, :mid], own[rows, mid:])
            for rows in (slice(k * quarter, (k + 1) * quarter) for k in (2 * side, 2 * side + 1))
        )
        low, high = halves(top, bottom)
        columns[side] = jnp.where(core == 0, low, high)
    for g in range(per_core):
        rows = pl.ds(pl.multiple_of((core * per_core + g) * BLK, BLK), BLK)
        scaled[g] = own[rows, :] * ritz[...]
        m_hi[g], m_lo[g] = split(jnp.concatenate([mats[g, q] for q in range(4)], 1))
    lane = lax.broadcasted_iota(jnp.int32, ids.shape, 1)
    value = jnp.zeros(ids.shape, jnp.int32)
    for p in range(4):
        value = jnp.where(lane == p, map_copy[0, p], value)
    ids[...] = value.astype(F32)


def residual_kernel(
    place, lists, halo, own_hi, own_lo, scaled, m_hi, m_lo, residual, r_hi, r_lo, ext_hi, ext_lo
):
    sub, core = place[0], place[1] % 2
    blocks, per_core = own_hi.shape[0], m_hi.shape[0]
    hi, lo = split(halo[...].reshape(HALO, BLK, halo.shape[1]))
    ext_hi[pl.ds(core * blocks, HALO)] = hi
    ext_lo[pl.ds(core * blocks, HALO)] = lo
    start = HALO - core * HALO
    ext_hi[pl.ds(start, blocks)] = own_hi[...]
    ext_lo[pl.ds(start, blocks)] = own_lo[...]
    for g in range(per_core):
        where = [lists[q, core * per_core + g] - sub * blocks + start for q in range(4)]
        rhs = [jnp.concatenate([e[w] for w in where], 0) for e in (ext_hi, ext_lo)]
        rows = slice(g * BLK, (g + 1) * BLK)
        res = dot3((m_hi[g], m_lo[g]), rhs) - scaled[g]
        residual[rows, :] = res
        r_hi[rows, :], r_lo[rows, :] = split(res)


def mine_kernel(place, e_hi, e_lo, r_hi, r_lo, sums):
    core = place[1] % 2
    sums[...] = dot3((e_hi[core], e_lo[core]), (r_hi[...], r_lo[...]))


def theirs_kernel(
    place, sums, theirs, e_hi, e_lo, m_hi, m_lo, ids, r_hi, r_lo, pieces
):
    core = place[1] % 2
    other = 1 - core
    hi, lo = split(theirs[...])
    r_hi[other], r_lo[other] = hi, lo
    r_hi[core], r_lo[core] = m_hi[...], m_lo[...]
    sep = e_hi.shape[1] // (2 * LOCAL)
    for k in range(2 * LOCAL):
        span = slice(k * sep, (k + 1) * sep)
        part = sums[span, :] + dot3((e_hi[other, span, :], e_lo[other, span, :]), (hi, lo))
        n, c = divmod(k, 2)
        for p in range(4):
            for h in range(2):
                row = ((c * 4 + p) * 2 + h) * 8
                tile = part[p * BLK : (p + 1) * BLK, h * LANES : (h + 1) * LANES]
                pieces[n * 16 : (n + 1) * 16, row : row + 8, :] = tile.reshape(16, 8, LANES)
    pieces[:, 128:136, :] = jnp.broadcast_to(ids[...][None], (32, 8, LANES))


def owner_kernel(place, maps, shift, received, back, total):
    sub = place[0]
    node = place[1] * LOCAL + sub // 16
    first_row = (sub % 16) * 8
    z_r, z_i, w_r, w_i = (constant(node, v) for v in (Z_REAL, Z_IMAG, W_REAL, W_IMAG))
    total[...] = jnp.zeros_like(total)

    def add(t, carry):
        for p in range(4):
            g = maps[t, p]
            for c in range(2):
                r = (c * 4 + p) * 16
                total[g, c] += received[t, r : r + 16, :]
        return carry

    lax.fori_loop(0, 32, add, 0, unroll=4)
    lane = lax.broadcasted_iota(jnp.int32, (8, LANES), 1)
    pick = lane == first_row + lax.broadcasted_iota(jnp.int32, (8, LANES), 0)
    for g in range(GROUPS):
        row = jnp.broadcast_to(shift[g : g + 1, :], (8, LANES))
        gap = z_r - jnp.sum(jnp.where(pick, row, 0.0), axis=1, keepdims=True)
        gap = jnp.concatenate([gap, gap], 0)
        modulus = gap * gap + z_i * z_i
        real, imag = total[g, 0], total[g, 1]
        c_r = (real * gap + imag * z_i) / modulus
        c_i = (imag * gap - real * z_i) / modulus
        total[g, 0] = w_r * c_r - w_i * c_i
        total[g, 1] = w_r * c_i + w_i * c_r

    def give(t, carry):
        for p in range(4):
            g = maps[t, p]
            for c in range(2):
                r = (c * 4 + p) * 16
                back[t, r : r + 16, :] = total[g, c]
        return carry

    lax.fori_loop(0, 32, give, 0, unroll=4)


def coarse_halves(picked, x_hi, x_lo):
    sep = x_hi.shape[0] // (2 * LOCAL)
    for k in range(2 * LOCAL):
        n, c = divmod(k, 2)
        for p in range(4):
            for h in range(2):
                row = ((c * 4 + p) * 2 + h) * 8
                tile = picked[n * 16 : (n + 1) * 16, row : row + 8, :].reshape(BLK, LANES)
                rows = slice(k * sep + p * BLK, k * sep + (p + 1) * BLK)
                cols = slice(h * LANES, (h + 1) * LANES)
                x_hi[rows, cols], x_lo[rows, cols] = split(tile)


def solve(side, core, coarse, f_hi, f_lo, r_hi, r_lo, w_hi, w_lo, keep, send):
    per_side = w_hi.shape[0] // 2
    quarters = []
    for g in range(0, per_side, 2):
        first = side * per_side + g
        both = slice(first * BLK, (first + 2) * BLK)
        back = dot3((f_hi[both, :], f_lo[both, :]), coarse)
        local = []
        for i in range(2):
            rows = slice((g + i) * BLK, (g + i + 1) * BLK)
            local.append(
                dot3((w_hi[first + i], w_lo[first + i]), (r_hi[side, rows, :], r_lo[side, rows, :]))
            )
        quarters.append(back + jnp.concatenate(local, 0))
    for chip in range(2):
        cols = slice(chip * LANES, (chip + 1) * LANES)
        low, high = halves(quarters[0][:, cols], quarters[1][:, cols])
        keep[chip] = jnp.where(core == 0, low, high)
        send[chip] = jnp.where(core == 0, high, low)


def first_kernel(place, picked, f_hi, f_lo, r_hi, r_lo, w_hi, w_lo, keep, send, x_hi, x_lo):
    coarse_halves(picked, x_hi, x_lo)
    coarse = x_hi[...], x_lo[...]
    solve(0, place[1] % 2, coarse, f_hi, f_lo, r_hi, r_lo, w_hi, w_lo, keep, send)


def second_kernel(place, x_hi, x_lo, f_hi, f_lo, r_hi, r_lo, w_hi, w_lo, keep, send):
    coarse = x_hi[...], x_lo[...]
    solve(1, place[1] % 2, coarse, f_hi, f_lo, r_hi, r_lo, w_hi, w_lo, keep, send)


def scale_kernel(rows, update_a, update_b, squares, out):
    quarter = update_a.shape[0]
    factor = lax.rsqrt(jnp.sum(squares[...], axis=0) / rows + 1e-06)
    for side, update in enumerate((update_a, update_b)):
        new = (update[...] * factor).T
        for h in range(2):
            start = (2 * side + h) * quarter
            out[:, start : start + quarter] = new[h * (LANES // 2) : (h + 1) * (LANES // 2)]


def call(body, name, specs, shapes, scratch=(), limit=16, flops=0):
    shapes = [s if isinstance(s, jax.ShapeDtypeStruct) else jax.ShapeDtypeStruct(s, F32) for s in shapes]
    return pl.pallas_call(
        body,
        name=name,
        in_specs=specs,
        out_specs=[VMEM] * len(shapes),
        out_shape=shapes,
        scratch_shapes=list(scratch),
        cost_estimate=pl.CostEstimate(flops=flops, bytes_accessed=8 << 20, transcendentals=0),
        compiler_params=pltpu.CompilerParams(vmem_limit_bytes=limit << 20),
    )


def shards(
    search_vectors,
    ritz_values,
    matrix_blocks,
    block_lists,
    inverses,
    panels,
    separator_map,
    separator_shift,
):
    rows, width = search_vectors.shape
    subs, nodes = lax.axis_size("sub"), lax.axis_size("node")
    sub, node = lax.axis_index("sub"), lax.axis_index("node")
    place = jnp.stack([sub, node]).astype(jnp.int32)

    halo_rows = HALO * BLK
    edge = lax.dynamic_slice_in_dim(
        search_vectors, jnp.where(node % 2 == 0, rows - halo_rows, 0), halo_rows, 0
    )
    ring = []
    for t in range(subs):
        for n in range(nodes):
            d = t + 1 if n % 2 == 0 else t - 1
            if 0 <= d < subs:
                ring.append((t * nodes + n, d * nodes + n))
    swap_core = [(i, i ^ 1) for i in range(nodes)]
    swap_chip = [(i, i ^ 2) for i in range(nodes)]
    halo = lax.ppermute(edge, ("sub", "node"), ring)

    half = functools.partial(jax.ShapeDtypeStruct, dtype=BF16)
    blocks, sep = rows // BLK, panels.shape[1]
    per_core = blocks // 2
    prepared = call(
        prepare_kernel,
        "prepare",
        [SMEM] + [HBM] * 6,
        [half((blocks, BLK, width))] * 2
        + [(per_core, BLK, width)]
        + [half((per_core, BLK, 4 * BLK))] * 2
        + [half((2, 4 * sep, rows // 2))] * 2
        + [half((rows, 4 * sep))] * 2
        + [half((blocks, BLK, BLK))] * 2
        + [(8, LANES), (2, rows // 4, LANES)],
        [
            pltpu.VMEM((rows, width), F32),
            pltpu.VMEM((1, width), F32),
            pltpu.VMEM((per_core, 4, BLK, BLK), F32),
            pltpu.VMEM((blocks, LOCAL, 2, BLK, BLK), F32),
            pltpu.VMEM((sep, rows), F32),
            pltpu.SemaphoreType.DMA,
            pltpu.SemaphoreType.DMA,
            pltpu.SemaphoreType.DMA,
            pltpu.SemaphoreType.DMA,
            pltpu.SemaphoreType.DMA((blocks, 2)),
            pltpu.SMEM(separator_map.shape, jnp.int32),
        ],
        limit=24,
        flops=8 * 10**9,
    )(
        place, *(
            pltpu.with_memory_space_constraint(x, pltpu.HBM)
            for x in (
                separator_map, search_vectors, ritz_values[None, :],
                matrix_blocks, inverses, panels,
            )
        )
    )
    own_hi, own_lo, scaled, m_hi, m_lo, e_hi, e_lo, f_hi, f_lo, w_hi, w_lo, ids, columns = prepared
    halo, ids = lax.optimization_barrier((halo, ids))
    residual, mine_hi, mine_lo = call(
        residual_kernel,
        "residual",
        [SMEM, SMEM] + [VMEM] * 6,
        [(rows // 2, width)] + [half((rows // 2, width))] * 2,
        [pltpu.VMEM((blocks + HALO, BLK, width), BF16)] * 2,
        flops=10**9,
    )(place, block_lists.T, halo, own_hi, own_lo, scaled, m_hi, m_lo)
    theirs = lax.ppermute(residual, "node", swap_core)
    (sums,) = call(
        mine_kernel,
        "mine",
        [SMEM] + [VMEM] * 4,
        [(4 * sep, width)],
        flops=4 * 10**9,
    )(place, e_hi, e_lo, mine_hi, mine_lo)
    theirs, sums = lax.optimization_barrier((theirs, sums))
    r_hi, r_lo, pieces = call(
        theirs_kernel,
        "theirs",
        [SMEM] + [VMEM] * 7,
        [half((2, rows // 2, width))] * 2 + [(subs, 136, LANES)],
        flops=4 * 10**9,
    )(place, sums, theirs, e_hi, e_lo, mine_hi, mine_lo, ids)
    received = lax.all_to_all(pieces, "sub", 0, 0, tiled=True)
    maps = received[:, 128, :4].astype(jnp.int32)
    (back,) = call(
        owner_kernel,
        "owner",
        [SMEM, SMEM, VMEM, VMEM],
        [(subs, 128, LANES)],
        [pltpu.VMEM((GROUPS, 2, 16, LANES), F32)],
    )(place, maps, separator_shift.reshape(GROUPS, LANES), received)
    picked = lax.all_to_all(back, "sub", 0, 0, tiled=True)
    operators = (f_hi, f_lo, r_hi, r_lo, w_hi, w_lo)
    keep_a, send_a, x_hi, x_lo = call(
        first_kernel,
        "first",
        [SMEM] + [VMEM] * 7,
        [(2, rows // 4, LANES)] * 2 + [half((4 * sep, width))] * 2,
        flops=2 * 10**9,
    )(place, picked, *operators)
    theirs_a = lax.ppermute(send_a, "node", swap_core)
    keep_b, send_b = call(
        second_kernel,
        "second",
        [SMEM] + [VMEM] * 8,
        [(2, rows // 4, LANES)] * 2,
        flops=2 * 10**9,
    )(place, x_hi, x_lo, *operators)
    theirs_a, send_b = lax.optimization_barrier((theirs_a, send_b))
    theirs_b = lax.ppermute(send_b, "node", swap_core)
    chip = node // 2

    def both(index, keep, theirs):
        return lax.dynamic_index_in_dim(keep, index, 0, False) + lax.dynamic_index_in_dim(
            theirs, index, 0, False
        )

    far_a = lax.ppermute(both(1 - chip, keep_a, theirs_a), "node", swap_chip)
    far_b = lax.ppermute(both(1 - chip, keep_b, theirs_b), "node", swap_chip)
    update_a = columns[0] - (both(chip, keep_a, theirs_a) + far_a)
    update_b = columns[1] - (both(chip, keep_b, theirs_b) + far_b)
    sums = jnp.sum(update_a * update_a, axis=0) + jnp.sum(update_b * update_b, axis=0)
    sums = sums + jnp.roll(sums, LANES // 2)
    squares = jnp.broadcast_to(sums[None, None], (subs, 1, LANES))
    gathered = lax.all_to_all(squares, "sub", 0, 0, tiled=True)
    (out,) = call(
        functools.partial(scale_kernel, rows * subs),
        "scale",
        [VMEM, VMEM, VMEM],
        [(width // nodes, rows)],
    )(update_a, update_b, gathered)
    return out.T


def solution(mesh):
    return jax.shard_map(
        shards,
        mesh=mesh,
        in_specs=(
            P("sub", None),
            P(),
            P("sub", None, None, None),
            P("sub", None),
            P("node", None, "sub", None, None),
            P("sub", None, None),
            P("sub", None),
            P(),
        ),
        out_specs=P("sub", "node"),
        check_vma=False,
    )
```

```python
import functools
import math

import jax
import jax.numpy as jnp
from jax import lax
from jax.experimental import pallas as pl
from jax.experimental.pallas import tpu as pltpu
from jax.sharding import PartitionSpec as P

BLK = 128
HALO = 4
GROUPS = 8
NODES = 8
LOCAL = 2
LANES = 128

F32 = jnp.float32
BF16 = jnp.bfloat16
VMEM = pl.BlockSpec(memory_space=pltpu.VMEM)
SMEM = pl.BlockSpec(memory_space=pltpu.SMEM)
HBM = pl.BlockSpec(memory_space=pltpu.HBM)

THETA = [math.pi * (j + 0.5) / NODES for j in range(NODES)]
Z_REAL, Z_IMAG = [math.cos(t) for t in THETA], [math.sin(t) for t in THETA]
W_REAL, W_IMAG = [2.0 * v / NODES for v in Z_REAL], [2.0 * v / NODES for v in Z_IMAG]


def split(x):
    hi = x.astype(BF16)
    return hi, (x - hi.astype(F32)).astype(BF16)


def dot(a, b, dims=((1,), (0,))):
    return lax.dot_general(a, b, (dims, ((), ())), preferred_element_type=F32)


def dot3(a, b, dims=((1,), (0,))):
    return dot(a[0], b[0], dims) + (dot(a[0], b[1], dims) + dot(a[1], b[0], dims))


def halves(top, bottom):
    low = lax.broadcasted_iota(jnp.int32, top.shape, 1) < LANES // 2
    return (
        jnp.where(low, top, pltpu.roll(bottom, LANES // 2, 1)),
        jnp.where(low, pltpu.roll(top, LANES // 2, 1), bottom),
    )


def constant(node, values):
    out = jnp.float32(values[0])
    for k in range(1, NODES):
        out = jnp.where(node == k, jnp.float32(values[k]), out)
    return out


def prepare_kernel(
    place, sep_map, own_hbm, ritz_hbm, mats_hbm, inverses_hbm, panel_hbm,
    own_hi, own_lo, scaled, m_hi, m_lo, e_hi, e_lo, f_hi, f_lo, w_hi, w_lo, ids, columns,
    own, ritz, mats, inverses, panel, ids_sem, ritz_sem, mats_sem, panel_sem, sems, map_copy,
):
    node, core = place[1] * LOCAL, place[1] % 2
    blocks, sep = own.shape[0] // BLK, panel.shape[0]
    per_core = blocks // 2
    parts = [(n, c) for n in range(LOCAL) for c in range(2)]
    copies = []
    for g in range(blocks):
        rows = pl.ds(g * BLK, BLK)
        copies.append(
            (
                pltpu.make_async_copy(inverses_hbm.at[:, :, g], inverses.at[g], sems.at[g, 0]),
                pltpu.make_async_copy(own_hbm.at[rows, :], own.at[rows, :], sems.at[g, 1]),
            )
        )
    my_mats = pltpu.make_async_copy(
        mats_hbm.at[pl.ds(core * per_core, per_core)], mats, mats_sem
    )
    whole_panel = pltpu.make_async_copy(panel_hbm.at[0], panel, panel_sem)
    small = [
        pltpu.make_async_copy(ritz_hbm, ritz, ritz_sem),
        pltpu.make_async_copy(sep_map, map_copy, ids_sem),
    ]
    for copy in [whole_panel, *copies[0], *sum(copies[1:], ()), my_mats] + small:
        copy.start()
    whole_panel.wait()
    for g in range(blocks):
        for copy in copies[g]:
            copy.wait()
        rows = slice(g * BLK, (g + 1) * BLK)
        own_hi[g], own_lo[g] = split(own[rows, :])
        weighted = []
        for n in range(LOCAL):
            weighted.append(inverses[g, n, 0] * constant(node + n, W_REAL))
            weighted.append(inverses[g, n, 1] * -constant(node + n, W_IMAG))
        w_hi[g], w_lo[g] = split(sum(weighted[1:], weighted[0]))
        p_hi, p_lo = split(panel[:, rows])
        d_hi, d_lo = split(jnp.concatenate([inverses[g, n, c] for n, c in parts], 1))
        e = dot(
            jnp.concatenate([p_hi, p_lo, p_hi], 1), jnp.concatenate([d_hi, d_hi, d_lo], 0)
        )
        d_hi, d_lo = split(
            jnp.concatenate([-inverses[g, n, c] if c == 0 else inverses[g, n, c] for n, c in parts], 0)
        )
        f = dot(
            jnp.concatenate([d_hi, d_lo, d_hi], 1),
            jnp.concatenate([p_hi, p_hi, p_lo], 1),
            ((1,), (1,)),
        )
        side, nth = divmod(g, per_core)
        cols = slice(nth * BLK, (nth + 1) * BLK)
        for k in range(2 * LOCAL):
            span, block = slice(k * sep, (k + 1) * sep), slice(k * BLK, (k + 1) * BLK)
            e_hi[side, span, cols], e_lo[side, span, cols] = split(e[:, block])
            f_hi[rows, span], f_lo[rows, span] = split(f[block, :])
    for copy in small:
        copy.wait()
    my_mats.wait()
    first, mid, quarter = place[1] // 2 == 0, own.shape[1] // 2, own.shape[0] // 4
    for side in range(2):
        top, bottom = (
            jnp.where(first, own[rows, :mid], own[rows, mid:])
            for rows in (slice(k * quarter, (k + 1) * quarter) for k in (2 * side, 2 * side + 1))
        )
        low, high = halves(top, bottom)
        columns[side] = jnp.where(core == 0, low, high)
    for g in range(per_core):
        rows = pl.ds(pl.multiple_of((core * per_core + g) * BLK, BLK), BLK)
        scaled[g] = own[rows, :] * ritz[...]
        m_hi[g], m_lo[g] = split(jnp.concatenate([mats[g, q] for q in range(4)], 1))
    lane = lax.broadcasted_iota(jnp.int32, ids.shape, 1)
    value = jnp.zeros(ids.shape, jnp.int32)
    for p in range(4):
        value = jnp.where(lane == p, map_copy[0, p], value)
    ids[...] = value.astype(F32)


def residual_kernel(
    place, lists, halo, own_hi, own_lo, scaled, m_hi, m_lo, residual, r_hi, r_lo, ext_hi, ext_lo
):
    sub, core = place[0], place[1] % 2
    blocks, per_core = own_hi.shape[0], m_hi.shape[0]
    hi, lo = split(halo[...].reshape(HALO, BLK, halo.shape[1]))
    ext_hi[pl.ds(core * blocks, HALO)] = hi
    ext_lo[pl.ds(core * blocks, HALO)] = lo
    start = HALO - core * HALO
    ext_hi[pl.ds(start, blocks)] = own_hi[...]
    ext_lo[pl.ds(start, blocks)] = own_lo[...]
    for g in range(per_core):
        where = [lists[q, core * per_core + g] - sub * blocks + start for q in range(4)]
        rhs = [jnp.concatenate([e[w] for w in where], 0) for e in (ext_hi, ext_lo)]
        rows = slice(g * BLK, (g + 1) * BLK)
        res = dot3((m_hi[g], m_lo[g]), rhs) - scaled[g]
        residual[rows, :] = res
        r_hi[rows, :], r_lo[rows, :] = split(res)


def mine_kernel(place, e_hi, e_lo, r_hi, r_lo, sums):
    core = place[1] % 2
    sums[...] = dot3((e_hi[core], e_lo[core]), (r_hi[...], r_lo[...]))


def theirs_kernel(
    place, sums, theirs, e_hi, e_lo, m_hi, m_lo, ids, r_hi, r_lo, pieces
):
    core = place[1] % 2
    other = 1 - core
    hi, lo = split(theirs[...])
    r_hi[other], r_lo[other] = hi, lo
    r_hi[core], r_lo[core] = m_hi[...], m_lo[...]
    sep = e_hi.shape[1] // (2 * LOCAL)
    for k in range(2 * LOCAL):
        span = slice(k * sep, (k + 1) * sep)
        part = sums[span, :] + dot3((e_hi[other, span, :], e_lo[other, span, :]), (hi, lo))
        n, c = divmod(k, 2)
        for p in range(4):
            for h in range(2):
                row = ((p * 2 + c) * 2 + h) * 8
                tile = part[p * BLK : (p + 1) * BLK, h * LANES : (h + 1) * LANES]
                pieces[n * 16 : (n + 1) * 16, row : row + 8, :] = tile.reshape(16, 8, LANES)
    pieces[:, 128:136, :] = jnp.broadcast_to(ids[...][None], (32, 8, LANES))


def owner_kernel(place, maps, shift, received, back, total):
    sub = place[0]
    node = place[1] * LOCAL + sub // 16
    first_row = (sub % 16) * 8
    z_r, z_i, w_r, w_i = (constant(node, v) for v in (Z_REAL, Z_IMAG, W_REAL, W_IMAG))
    total[...] = jnp.zeros_like(total)

    def add(t, carry):
        groups = [maps[t, p] for p in range(4)]
        sums = [total[g] + received[t, p * 32 : (p + 1) * 32, :] for p, g in enumerate(groups)]
        for g, value in zip(groups, sums):
            total[g] = value
        return carry

    lax.fori_loop(0, 32, add, 0, unroll=4)
    lane = lax.broadcasted_iota(jnp.int32, (8, LANES), 1)
    pick = lane == first_row + lax.broadcasted_iota(jnp.int32, (8, LANES), 0)
    for g in range(GROUPS):
        row = jnp.broadcast_to(shift[g : g + 1, :], (8, LANES))
        gap = z_r - jnp.sum(jnp.where(pick, row, 0.0), axis=1, keepdims=True)
        gap = jnp.concatenate([gap, gap], 0)
        modulus = gap * gap + z_i * z_i
        real, imag = total[g, :16], total[g, 16:]
        c_r = (real * gap + imag * z_i) / modulus
        c_i = (imag * gap - real * z_i) / modulus
        total[g, :16] = w_r * c_r - w_i * c_i
        total[g, 16:] = w_r * c_i + w_i * c_r

    def give(t, carry):
        for p in range(4):
            back[t, p * 32 : (p + 1) * 32, :] = total[maps[t, p]]
        return carry

    lax.fori_loop(0, 32, give, 0, unroll=4)


def coarse_halves(picked, x_hi, x_lo):
    sep = x_hi.shape[0] // (2 * LOCAL)
    for k in range(2 * LOCAL):
        n, c = divmod(k, 2)
        for p in range(4):
            for h in range(2):
                row = ((p * 2 + c) * 2 + h) * 8
                tile = picked[n * 16 : (n + 1) * 16, row : row + 8, :].reshape(BLK, LANES)
                rows = slice(k * sep + p * BLK, k * sep + (p + 1) * BLK)
                cols = slice(h * LANES, (h + 1) * LANES)
                x_hi[rows, cols], x_lo[rows, cols] = split(tile)


def solve(side, core, coarse, f_hi, f_lo, r_hi, r_lo, w_hi, w_lo, keep, send):
    per_side = w_hi.shape[0] // 2
    quarters = []
    for g in range(0, per_side, 2):
        first = side * per_side + g
        both = slice(first * BLK, (first + 2) * BLK)
        back = dot3((f_hi[both, :], f_lo[both, :]), coarse)
        local = []
        for i in range(2):
            rows = slice((g + i) * BLK, (g + i + 1) * BLK)
            local.append(
                dot3((w_hi[first + i], w_lo[first + i]), (r_hi[side, rows, :], r_lo[side, rows, :]))
            )
        quarters.append(back + jnp.concatenate(local, 0))
    for chip in range(2):
        cols = slice(chip * LANES, (chip + 1) * LANES)
        low, high = halves(quarters[0][:, cols], quarters[1][:, cols])
        keep[chip] = jnp.where(core == 0, low, high)
        send[chip] = jnp.where(core == 0, high, low)


def first_kernel(place, picked, f_hi, f_lo, r_hi, r_lo, w_hi, w_lo, keep, send, x_hi, x_lo):
    coarse_halves(picked, x_hi, x_lo)
    coarse = x_hi[...], x_lo[...]
    solve(0, place[1] % 2, coarse, f_hi, f_lo, r_hi, r_lo, w_hi, w_lo, keep, send)


def second_kernel(place, x_hi, x_lo, f_hi, f_lo, r_hi, r_lo, w_hi, w_lo, keep, send):
    coarse = x_hi[...], x_lo[...]
    solve(1, place[1] % 2, coarse, f_hi, f_lo, r_hi, r_lo, w_hi, w_lo, keep, send)


def scale_kernel(rows, update_a, update_b, squares, out):
    quarter = update_a.shape[0]
    factor = lax.rsqrt(jnp.sum(squares[...], axis=0) / rows + 1e-06)
    for side, update in enumerate((update_a, update_b)):
        new = (update[...] * factor).T
        for h in range(2):
            start = (2 * side + h) * quarter
            out[:, start : start + quarter] = new[h * (LANES // 2) : (h + 1) * (LANES // 2)]


def call(body, name, specs, shapes, scratch=(), limit=16, flops=0):
    shapes = [s if isinstance(s, jax.ShapeDtypeStruct) else jax.ShapeDtypeStruct(s, F32) for s in shapes]
    return pl.pallas_call(
        body,
        name=name,
        in_specs=specs,
        out_specs=[VMEM] * len(shapes),
        out_shape=shapes,
        scratch_shapes=list(scratch),
        cost_estimate=pl.CostEstimate(flops=flops, bytes_accessed=8 << 20, transcendentals=0),
        compiler_params=pltpu.CompilerParams(vmem_limit_bytes=limit << 20),
    )


def shards(
    search_vectors,
    ritz_values,
    matrix_blocks,
    block_lists,
    inverses,
    panels,
    separator_map,
    separator_shift,
):
    rows, width = search_vectors.shape
    subs, nodes = lax.axis_size("sub"), lax.axis_size("node")
    sub, node = lax.axis_index("sub"), lax.axis_index("node")
    place = jnp.stack([sub, node]).astype(jnp.int32)

    halo_rows = HALO * BLK
    edge = lax.dynamic_slice_in_dim(
        search_vectors, jnp.where(node % 2 == 0, rows - halo_rows, 0), halo_rows, 0
    )
    ring = []
    for t in range(subs):
        for n in range(nodes):
            d = t + 1 if n % 2 == 0 else t - 1
            if 0 <= d < subs:
                ring.append((t * nodes + n, d * nodes + n))
    swap_core = [(i, i ^ 1) for i in range(nodes)]
    swap_chip = [(i, i ^ 2) for i in range(nodes)]
    halo = lax.ppermute(edge, ("sub", "node"), ring)

    half = functools.partial(jax.ShapeDtypeStruct, dtype=BF16)
    blocks, sep = rows // BLK, panels.shape[1]
    per_core = blocks // 2
    prepared = call(
        prepare_kernel,
        "prepare",
        [SMEM] + [HBM] * 6,
        [half((blocks, BLK, width))] * 2
        + [(per_core, BLK, width)]
        + [half((per_core, BLK, 4 * BLK))] * 2
        + [half((2, 4 * sep, rows // 2))] * 2
        + [half((rows, 4 * sep))] * 2
        + [half((blocks, BLK, BLK))] * 2
        + [(8, LANES), (2, rows // 4, LANES)],
        [
            pltpu.VMEM((rows, width), F32),
            pltpu.VMEM((1, width), F32),
            pltpu.VMEM((per_core, 4, BLK, BLK), F32),
            pltpu.VMEM((blocks, LOCAL, 2, BLK, BLK), F32),
            pltpu.VMEM((sep, rows), F32),
            pltpu.SemaphoreType.DMA,
            pltpu.SemaphoreType.DMA,
            pltpu.SemaphoreType.DMA,
            pltpu.SemaphoreType.DMA,
            pltpu.SemaphoreType.DMA((blocks, 2)),
            pltpu.SMEM(separator_map.shape, jnp.int32),
        ],
        limit=24,
        flops=8 * 10**9,
    )(
        place, *(
            pltpu.with_memory_space_constraint(x, pltpu.HBM)
            for x in (
                separator_map, search_vectors, ritz_values[None, :],
                matrix_blocks, inverses, panels,
            )
        )
    )
    own_hi, own_lo, scaled, m_hi, m_lo, e_hi, e_lo, f_hi, f_lo, w_hi, w_lo, ids, columns = prepared
    halo, ids = lax.optimization_barrier((halo, ids))
    residual, mine_hi, mine_lo = call(
        residual_kernel,
        "residual",
        [SMEM, SMEM] + [VMEM] * 6,
        [(rows // 2, width)] + [half((rows // 2, width))] * 2,
        [pltpu.VMEM((blocks + HALO, BLK, width), BF16)] * 2,
        flops=10**9,
    )(place, block_lists.T, halo, own_hi, own_lo, scaled, m_hi, m_lo)
    theirs = lax.ppermute(residual, "node", swap_core)
    (sums,) = call(
        mine_kernel,
        "mine",
        [SMEM] + [VMEM] * 4,
        [(4 * sep, width)],
        flops=4 * 10**9,
    )(place, e_hi, e_lo, mine_hi, mine_lo)
    theirs, sums = lax.optimization_barrier((theirs, sums))
    r_hi, r_lo, pieces = call(
        theirs_kernel,
        "theirs",
        [SMEM] + [VMEM] * 7,
        [half((2, rows // 2, width))] * 2 + [(subs, 136, LANES)],
        flops=4 * 10**9,
    )(place, sums, theirs, e_hi, e_lo, mine_hi, mine_lo, ids)
    received = lax.all_to_all(pieces, "sub", 0, 0, tiled=True)
    maps = received[:, 128, :4].astype(jnp.int32)
    (back,) = call(
        owner_kernel,
        "owner",
        [SMEM, SMEM, VMEM, VMEM],
        [(subs, 128, LANES)],
        [pltpu.VMEM((GROUPS, 32, LANES), F32)],
    )(place, maps, separator_shift.reshape(GROUPS, LANES), received)
    picked = lax.all_to_all(back, "sub", 0, 0, tiled=True)
    operators = (f_hi, f_lo, r_hi, r_lo, w_hi, w_lo)
    keep_a, send_a, x_hi, x_lo = call(
        first_kernel,
        "first",
        [SMEM] + [VMEM] * 7,
        [(2, rows // 4, LANES)] * 2 + [half((4 * sep, width))] * 2,
        flops=2 * 10**9,
    )(place, picked, *operators)
    theirs_a = lax.ppermute(send_a, "node", swap_core)
    keep_b, send_b = call(
        second_kernel,
        "second",
        [SMEM] + [VMEM] * 8,
        [(2, rows // 4, LANES)] * 2,
        flops=2 * 10**9,
    )(place, x_hi, x_lo, *operators)
    theirs_a, send_b = lax.optimization_barrier((theirs_a, send_b))
    theirs_b = lax.ppermute(send_b, "node", swap_core)
    chip = node // 2

    def both(index, keep, theirs):
        return lax.dynamic_index_in_dim(keep, index, 0, False) + lax.dynamic_index_in_dim(
            theirs, index, 0, False
        )

    far_a = lax.ppermute(both(1 - chip, keep_a, theirs_a), "node", swap_chip)
    far_b = lax.ppermute(both(1 - chip, keep_b, theirs_b), "node", swap_chip)
    update_a = columns[0] - (both(chip, keep_a, theirs_a) + far_a)
    update_b = columns[1] - (both(chip, keep_b, theirs_b) + far_b)
    sums = jnp.sum(update_a * update_a, axis=0) + jnp.sum(update_b * update_b, axis=0)
    sums = sums + jnp.roll(sums, LANES // 2)
    squares = jnp.broadcast_to(sums[None, None], (subs, 1, LANES))
    gathered = lax.all_to_all(squares, "sub", 0, 0, tiled=True)
    (out,) = call(
        functools.partial(scale_kernel, rows * subs),
        "scale",
        [VMEM, VMEM, VMEM],
        [(width // nodes, rows)],
    )(update_a, update_b, gathered)
    return out.T


def solution(mesh):
    return jax.shard_map(
        shards,
        mesh=mesh,
        in_specs=(
            P("sub", None),
            P(),
            P("sub", None, None, None),
            P("sub", None),
            P("node", None, "sub", None, None),
            P("sub", None, None),
            P("sub", None),
            P(),
        ),
        out_specs=P("sub", "node"),
        check_vma=False,
    )
```

```python
import functools
import math

import jax
import jax.numpy as jnp
from jax import lax
from jax.experimental import pallas as pl
from jax.experimental.pallas import tpu as pltpu
from jax.sharding import PartitionSpec as P

BLK = 128
HALO = 4
GROUPS = 8
NODES = 8
LOCAL = 2
LANES = 128

F32 = jnp.float32
BF16 = jnp.bfloat16
VMEM = pl.BlockSpec(memory_space=pltpu.VMEM)
SMEM = pl.BlockSpec(memory_space=pltpu.SMEM)
HBM = pl.BlockSpec(memory_space=pltpu.HBM)

THETA = [math.pi * (j + 0.5) / NODES for j in range(NODES)]
Z_REAL, Z_IMAG = [math.cos(t) for t in THETA], [math.sin(t) for t in THETA]
W_REAL, W_IMAG = [2.0 * v / NODES for v in Z_REAL], [2.0 * v / NODES for v in Z_IMAG]


def split(x):
    hi = x.astype(BF16)
    return hi, (x - hi.astype(F32)).astype(BF16)


def dot(a, b, dims=((1,), (0,))):
    return lax.dot_general(a, b, (dims, ((), ())), preferred_element_type=F32)


def dot3(a, b, dims=((1,), (0,))):
    return dot(a[0], b[0], dims) + (dot(a[0], b[1], dims) + dot(a[1], b[0], dims))


def halves(top, bottom):
    low = lax.broadcasted_iota(jnp.int32, top.shape, 1) < LANES // 2
    return (
        jnp.where(low, top, pltpu.roll(bottom, LANES // 2, 1)),
        jnp.where(low, pltpu.roll(top, LANES // 2, 1), bottom),
    )


def constant(node, values):
    out = jnp.float32(values[0])
    for k in range(1, NODES):
        out = jnp.where(node == k, jnp.float32(values[k]), out)
    return out


def prepare_kernel(
    place, sep_map, own_hbm, ritz_hbm, mats_hbm, inverses_hbm, panel_hbm,
    own_hi, own_lo, scaled, m_hi, m_lo, e_hi, e_lo, f_hi, f_lo, w_hi, w_lo, ids, columns,
    own, ritz, mats, inverses, panel, ids_sem, ritz_sem, mats_sem, panel_sem, sems, map_copy,
):
    node, core, side_of = place[1] * LOCAL, place[1] % 2, place[2]
    blocks, sep = own.shape[0] // BLK, panel.shape[0]
    per_core = blocks // 2
    parts = [(n, c) for n in range(LOCAL) for c in range(2)]
    copies = []
    for g in range(blocks):
        rows = pl.ds(g * BLK, BLK)
        copies.append(
            (
                pltpu.make_async_copy(inverses_hbm.at[:, :, g], inverses.at[g], sems.at[g, 0]),
                pltpu.make_async_copy(own_hbm.at[rows, :], own.at[rows, :], sems.at[g, 1]),
            )
        )
    my_mats = pltpu.make_async_copy(
        mats_hbm.at[pl.ds(side_of * per_core, per_core)], mats, mats_sem
    )
    whole_panel = pltpu.make_async_copy(panel_hbm.at[0], panel, panel_sem)
    small = [
        pltpu.make_async_copy(ritz_hbm, ritz, ritz_sem),
        pltpu.make_async_copy(sep_map, map_copy, ids_sem),
    ]
    for copy in [whole_panel, *copies[0], *sum(copies[1:], ()), my_mats] + small:
        copy.start()
    whole_panel.wait()
    for g in range(blocks):
        for copy in copies[g]:
            copy.wait()
        rows = slice(g * BLK, (g + 1) * BLK)
        own_hi[g], own_lo[g] = split(own[rows, :])
        weighted = []
        for n in range(LOCAL):
            weighted.append(inverses[g, n, 0] * constant(node + n, W_REAL))
            weighted.append(inverses[g, n, 1] * -constant(node + n, W_IMAG))
        w_hi[g], w_lo[g] = split(sum(weighted[1:], weighted[0]))
        p_hi, p_lo = split(panel[:, rows])
        d_hi, d_lo = split(jnp.concatenate([inverses[g, n, c] for n, c in parts], 1))
        e = dot(
            jnp.concatenate([p_hi, p_lo, p_hi], 1), jnp.concatenate([d_hi, d_hi, d_lo], 0)
        )
        d_hi, d_lo = split(
            jnp.concatenate([-inverses[g, n, c] if c == 0 else inverses[g, n, c] for n, c in parts], 0)
        )
        f = dot(
            jnp.concatenate([d_hi, d_lo, d_hi], 1),
            jnp.concatenate([p_hi, p_hi, p_lo], 1),
            ((1,), (1,)),
        )
        side, nth = divmod(g, per_core)
        cols = slice(nth * BLK, (nth + 1) * BLK)
        for k in range(2 * LOCAL):
            span, block = slice(k * sep, (k + 1) * sep), slice(k * BLK, (k + 1) * BLK)
            e_hi[side, span, cols], e_lo[side, span, cols] = split(e[:, block])
            f_hi[rows, span], f_lo[rows, span] = split(f[block, :])
    for copy in small:
        copy.wait()
    my_mats.wait()
    first, mid, quarter = place[1] // 2 == 0, own.shape[1] // 2, own.shape[0] // 4
    for side in range(2):
        top, bottom = (
            jnp.where(first, own[rows, :mid], own[rows, mid:])
            for rows in (slice(k * quarter, (k + 1) * quarter) for k in (2 * side, 2 * side + 1))
        )
        low, high = halves(top, bottom)
        columns[side] = jnp.where(core == 0, low, high)
    for g in range(per_core):
        rows = pl.ds(pl.multiple_of((side_of * per_core + g) * BLK, BLK), BLK)
        scaled[g] = own[rows, :] * ritz[...]
        m_hi[g], m_lo[g] = split(jnp.concatenate([mats[g, q] for q in range(4)], 1))
    lane = lax.broadcasted_iota(jnp.int32, ids.shape, 1)
    value = jnp.zeros(ids.shape, jnp.int32)
    for p in range(4):
        value = jnp.where(lane == p, map_copy[0, p], value)
    ids[...] = value.astype(F32)


def residual_kernel(
    place, lists, halo, own_hi, own_lo, scaled, m_hi, m_lo, residual, r_hi, r_lo, ext_hi, ext_lo
):
    sub, side = place[0], place[2]
    blocks, per_core = own_hi.shape[0], m_hi.shape[0]
    hi, lo = split(halo[...].reshape(HALO, BLK, halo.shape[1]))
    ext_hi[pl.ds(side * blocks, HALO)] = hi
    ext_lo[pl.ds(side * blocks, HALO)] = lo
    start = HALO - side * HALO
    ext_hi[pl.ds(start, blocks)] = own_hi[...]
    ext_lo[pl.ds(start, blocks)] = own_lo[...]
    for g in range(per_core):
        where = [lists[q, side * per_core + g] - sub * blocks + start for q in range(4)]
        rhs = [jnp.concatenate([e[w] for w in where], 0) for e in (ext_hi, ext_lo)]
        rows = slice(g * BLK, (g + 1) * BLK)
        res = dot3((m_hi[g], m_lo[g]), rhs) - scaled[g]
        residual[rows, :] = res
        r_hi[rows, :], r_lo[rows, :] = split(res)


def mine_kernel(place, e_hi, e_lo, r_hi, r_lo, sums):
    side = place[2]
    sums[...] = dot3((e_hi[side], e_lo[side]), (r_hi[...], r_lo[...]))


def theirs_kernel(
    place, sums, theirs, e_hi, e_lo, m_hi, m_lo, ids, r_hi, r_lo, pieces
):
    side = place[2]
    other = 1 - side
    hi, lo = split(theirs[...])
    r_hi[other], r_lo[other] = hi, lo
    r_hi[side], r_lo[side] = m_hi[...], m_lo[...]
    sep = e_hi.shape[1] // (2 * LOCAL)
    for k in range(2 * LOCAL):
        span = slice(k * sep, (k + 1) * sep)
        part = sums[span, :] + dot3((e_hi[other, span, :], e_lo[other, span, :]), (hi, lo))
        n, c = divmod(k, 2)
        for p in range(4):
            for h in range(2):
                row = ((p * 2 + c) * 2 + h) * 8
                tile = part[p * BLK : (p + 1) * BLK, h * LANES : (h + 1) * LANES]
                pieces[n * 16 : (n + 1) * 16, row : row + 8, :] = tile.reshape(16, 8, LANES)
    pieces[:, 128:136, :] = jnp.broadcast_to(ids[...][None], (32, 8, LANES))


def owner_kernel(place, maps, shift, received, back, total):
    sub = place[0]
    node = place[1] * LOCAL + sub // 16
    first_row = (sub % 16) * 8
    z_r, z_i, w_r, w_i = (constant(node, v) for v in (Z_REAL, Z_IMAG, W_REAL, W_IMAG))
    total[...] = jnp.zeros_like(total)

    def add(t, carry):
        groups = [maps[t, p] for p in range(4)]
        sums = [total[g] + received[t, p * 32 : (p + 1) * 32, :] for p, g in enumerate(groups)]
        for g, value in zip(groups, sums):
            total[g] = value
        return carry

    lax.fori_loop(0, 32, add, 0, unroll=4)
    lane = lax.broadcasted_iota(jnp.int32, (8, LANES), 1)
    pick = lane == first_row + lax.broadcasted_iota(jnp.int32, (8, LANES), 0)
    for g in range(GROUPS):
        row = jnp.broadcast_to(shift[g : g + 1, :], (8, LANES))
        gap = z_r - jnp.sum(jnp.where(pick, row, 0.0), axis=1, keepdims=True)
        gap = jnp.concatenate([gap, gap], 0)
        modulus = gap * gap + z_i * z_i
        real, imag = total[g, :16], total[g, 16:]
        c_r = (real * gap + imag * z_i) / modulus
        c_i = (imag * gap - real * z_i) / modulus
        total[g, :16] = w_r * c_r - w_i * c_i
        total[g, 16:] = w_r * c_i + w_i * c_r

    def give(t, carry):
        for p in range(4):
            back[t, p * 32 : (p + 1) * 32, :] = total[maps[t, p]]
        return carry

    lax.fori_loop(0, 32, give, 0, unroll=4)


def coarse_halves(picked, x_hi, x_lo):
    sep = x_hi.shape[0] // (2 * LOCAL)
    for k in range(2 * LOCAL):
        n, c = divmod(k, 2)
        for p in range(4):
            for h in range(2):
                row = ((p * 2 + c) * 2 + h) * 8
                tile = picked[n * 16 : (n + 1) * 16, row : row + 8, :].reshape(BLK, LANES)
                rows = slice(k * sep + p * BLK, k * sep + (p + 1) * BLK)
                cols = slice(h * LANES, (h + 1) * LANES)
                x_hi[rows, cols], x_lo[rows, cols] = split(tile)


def solve(side, core, coarse, f_hi, f_lo, r_hi, r_lo, w_hi, w_lo, keep, send):
    per_side = w_hi.shape[0] // 2
    quarters = []
    for g in range(0, per_side, 2):
        first = side * per_side + g
        both = slice(first * BLK, (first + 2) * BLK)
        back = dot3((f_hi[both, :], f_lo[both, :]), coarse)
        local = []
        for i in range(2):
            rows = slice((g + i) * BLK, (g + i + 1) * BLK)
            local.append(
                dot3((w_hi[first + i], w_lo[first + i]), (r_hi[side, rows, :], r_lo[side, rows, :]))
            )
        quarters.append(back + jnp.concatenate(local, 0))
    for chip in range(2):
        cols = slice(chip * LANES, (chip + 1) * LANES)
        low, high = halves(quarters[0][:, cols], quarters[1][:, cols])
        keep[chip] = jnp.where(core == 0, low, high)
        send[chip] = jnp.where(core == 0, high, low)


def first_kernel(place, picked, f_hi, f_lo, r_hi, r_lo, w_hi, w_lo, keep, send, x_hi, x_lo):
    coarse_halves(picked, x_hi, x_lo)
    coarse = x_hi[...], x_lo[...]
    solve(0, place[1] % 2, coarse, f_hi, f_lo, r_hi, r_lo, w_hi, w_lo, keep, send)


def second_kernel(place, x_hi, x_lo, f_hi, f_lo, r_hi, r_lo, w_hi, w_lo, keep, send):
    coarse = x_hi[...], x_lo[...]
    solve(1, place[1] % 2, coarse, f_hi, f_lo, r_hi, r_lo, w_hi, w_lo, keep, send)


def scale_kernel(rows, update_a, update_b, squares, out):
    quarter = update_a.shape[0]
    factor = lax.rsqrt(jnp.sum(squares[...], axis=0) / rows + 1e-06)
    for side, update in enumerate((update_a, update_b)):
        new = (update[...] * factor).T
        for h in range(2):
            start = (2 * side + h) * quarter
            out[:, start : start + quarter] = new[h * (LANES // 2) : (h + 1) * (LANES // 2)]


def call(body, name, specs, shapes, scratch=(), limit=16, flops=0):
    shapes = [s if isinstance(s, jax.ShapeDtypeStruct) else jax.ShapeDtypeStruct(s, F32) for s in shapes]
    return pl.pallas_call(
        body,
        name=name,
        in_specs=specs,
        out_specs=[VMEM] * len(shapes),
        out_shape=shapes,
        scratch_shapes=list(scratch),
        cost_estimate=pl.CostEstimate(flops=flops, bytes_accessed=8 << 20, transcendentals=0),
        compiler_params=pltpu.CompilerParams(vmem_limit_bytes=limit << 20),
    )


def shards(
    search_vectors,
    ritz_values,
    matrix_blocks,
    block_lists,
    inverses,
    panels,
    separator_map,
    separator_shift,
):
    rows, width = search_vectors.shape
    subs, nodes = lax.axis_size("sub"), lax.axis_size("node")
    sub, node = lax.axis_index("sub"), lax.axis_index("node")
    side = (node + sub) % 2
    place = jnp.stack([sub, node, side]).astype(jnp.int32)

    halo_rows = HALO * BLK
    edge = lax.dynamic_slice_in_dim(
        search_vectors, jnp.where(side == 0, rows - halo_rows, 0), halo_rows, 0
    )
    ring = []
    for t in range(subs):
        for n in range(nodes):
            d = t + 1 if (n + t) % 2 == 0 else t - 1
            if 0 <= d < subs:
                ring.append((t * nodes + n, d * nodes + (n ^ 3)))
    swap_core = [(i, i ^ 1) for i in range(nodes)]
    swap_chip = [(i, i ^ 2) for i in range(nodes)]
    halo = lax.ppermute(edge, ("sub", "node"), ring)

    half = functools.partial(jax.ShapeDtypeStruct, dtype=BF16)
    blocks, sep = rows // BLK, panels.shape[1]
    per_core = blocks // 2
    prepared = call(
        prepare_kernel,
        "prepare",
        [SMEM] + [HBM] * 6,
        [half((blocks, BLK, width))] * 2
        + [(per_core, BLK, width)]
        + [half((per_core, BLK, 4 * BLK))] * 2
        + [half((2, 4 * sep, rows // 2))] * 2
        + [half((rows, 4 * sep))] * 2
        + [half((blocks, BLK, BLK))] * 2
        + [(8, LANES), (2, rows // 4, LANES)],
        [
            pltpu.VMEM((rows, width), F32),
            pltpu.VMEM((1, width), F32),
            pltpu.VMEM((per_core, 4, BLK, BLK), F32),
            pltpu.VMEM((blocks, LOCAL, 2, BLK, BLK), F32),
            pltpu.VMEM((sep, rows), F32),
            pltpu.SemaphoreType.DMA,
            pltpu.SemaphoreType.DMA,
            pltpu.SemaphoreType.DMA,
            pltpu.SemaphoreType.DMA,
            pltpu.SemaphoreType.DMA((blocks, 2)),
            pltpu.SMEM(separator_map.shape, jnp.int32),
        ],
        limit=24,
        flops=8 * 10**9,
    )(
        place, *(
            pltpu.with_memory_space_constraint(x, pltpu.HBM)
            for x in (
                separator_map, search_vectors, ritz_values[None, :],
                matrix_blocks, inverses, panels,
            )
        )
    )
    own_hi, own_lo, scaled, m_hi, m_lo, e_hi, e_lo, f_hi, f_lo, w_hi, w_lo, ids, columns = prepared
    halo, ids = lax.optimization_barrier((halo, ids))
    residual, mine_hi, mine_lo = call(
        residual_kernel,
        "residual",
        [SMEM, SMEM] + [VMEM] * 6,
        [(rows // 2, width)] + [half((rows // 2, width))] * 2,
        [pltpu.VMEM((blocks + HALO, BLK, width), BF16)] * 2,
        flops=10**9,
    )(place, block_lists.T, halo, own_hi, own_lo, scaled, m_hi, m_lo)
    theirs = lax.ppermute(residual, "node", swap_core)
    (sums,) = call(
        mine_kernel,
        "mine",
        [SMEM] + [VMEM] * 4,
        [(4 * sep, width)],
        flops=4 * 10**9,
    )(place, e_hi, e_lo, mine_hi, mine_lo)
    theirs, sums = lax.optimization_barrier((theirs, sums))
    r_hi, r_lo, pieces = call(
        theirs_kernel,
        "theirs",
        [SMEM] + [VMEM] * 7,
        [half((2, rows // 2, width))] * 2 + [(subs, 136, LANES)],
        flops=4 * 10**9,
    )(place, sums, theirs, e_hi, e_lo, mine_hi, mine_lo, ids)
    received = lax.all_to_all(pieces, "sub", 0, 0, tiled=True)
    maps = received[:, 128, :4].astype(jnp.int32)
    (back,) = call(
        owner_kernel,
        "owner",
        [SMEM, SMEM, VMEM, VMEM],
        [(subs, 128, LANES)],
        [pltpu.VMEM((GROUPS, 32, LANES), F32)],
    )(place, maps, separator_shift.reshape(GROUPS, LANES), received)
    picked = lax.all_to_all(back, "sub", 0, 0, tiled=True)
    operators = (f_hi, f_lo, r_hi, r_lo, w_hi, w_lo)
    keep_a, send_a, x_hi, x_lo = call(
        first_kernel,
        "first",
        [SMEM] + [VMEM] * 7,
        [(2, rows // 4, LANES)] * 2 + [half((4 * sep, width))] * 2,
        flops=2 * 10**9,
    )(place, picked, *operators)
    theirs_a = lax.ppermute(send_a, "node", swap_core)
    keep_b, send_b = call(
        second_kernel,
        "second",
        [SMEM] + [VMEM] * 8,
        [(2, rows // 4, LANES)] * 2,
        flops=2 * 10**9,
    )(place, x_hi, x_lo, *operators)
    theirs_a, send_b = lax.optimization_barrier((theirs_a, send_b))
    theirs_b = lax.ppermute(send_b, "node", swap_core)
    chip = node // 2

    def both(index, keep, theirs):
        return lax.dynamic_index_in_dim(keep, index, 0, False) + lax.dynamic_index_in_dim(
            theirs, index, 0, False
        )

    far_a = lax.ppermute(both(1 - chip, keep_a, theirs_a), "node", swap_chip)
    far_b = lax.ppermute(both(1 - chip, keep_b, theirs_b), "node", swap_chip)
    update_a = columns[0] - (both(chip, keep_a, theirs_a) + far_a)
    update_b = columns[1] - (both(chip, keep_b, theirs_b) + far_b)
    sums = jnp.sum(update_a * update_a, axis=0) + jnp.sum(update_b * update_b, axis=0)
    sums = sums + jnp.roll(sums, LANES // 2)
    squares = jnp.broadcast_to(sums[None, None], (subs, 1, LANES))
    gathered = lax.all_to_all(squares, "sub", 0, 0, tiled=True)
    (out,) = call(
        functools.partial(scale_kernel, rows * subs),
        "scale",
        [VMEM, VMEM, VMEM],
        [(width // nodes, rows)],
    )(update_a, update_b, gathered)
    return out.T


def solution(mesh):
    return jax.shard_map(
        shards,
        mesh=mesh,
        in_specs=(
            P("sub", None),
            P(),
            P("sub", None, None, None),
            P("sub", None),
            P("node", None, "sub", None, None),
            P("sub", None, None),
            P("sub", None),
            P(),
        ),
        out_specs=P("sub", "node"),
        check_vma=False,
    )
```

```python
import functools
import math

import jax
import jax.numpy as jnp
from jax import lax
from jax.experimental import pallas as pl
from jax.experimental.pallas import tpu as pltpu
from jax.sharding import PartitionSpec as P

BLK = 128
HALO = 4
GROUPS = 8
NODES = 8
LOCAL = 2
LANES = 128

F32 = jnp.float32
BF16 = jnp.bfloat16
VMEM = pl.BlockSpec(memory_space=pltpu.VMEM)
SMEM = pl.BlockSpec(memory_space=pltpu.SMEM)
HBM = pl.BlockSpec(memory_space=pltpu.HBM)

THETA = [math.pi * (j + 0.5) / NODES for j in range(NODES)]
Z_REAL, Z_IMAG = [math.cos(t) for t in THETA], [math.sin(t) for t in THETA]
W_REAL, W_IMAG = [2.0 * v / NODES for v in Z_REAL], [2.0 * v / NODES for v in Z_IMAG]


def split(x):
    hi = x.astype(BF16)
    return hi, (x - hi.astype(F32)).astype(BF16)


def dot(a, b, dims=((1,), (0,))):
    return lax.dot_general(a, b, (dims, ((), ())), preferred_element_type=F32)


def dot3(a, b, dims=((1,), (0,))):
    return dot(a[0], b[0], dims) + (dot(a[0], b[1], dims) + dot(a[1], b[0], dims))


def halves(top, bottom):
    low = lax.broadcasted_iota(jnp.int32, top.shape, 1) < LANES // 2
    return (
        jnp.where(low, top, pltpu.roll(bottom, LANES // 2, 1)),
        jnp.where(low, pltpu.roll(top, LANES // 2, 1), bottom),
    )


def constant(node, values):
    out = jnp.float32(values[0])
    for k in range(1, NODES):
        out = jnp.where(node == k, jnp.float32(values[k]), out)
    return out


def prepare_kernel(
    place, sep_map, own_hbm, ritz_hbm, mats_hbm, inverses_hbm, panel_hbm,
    own_hi, own_lo, scaled, m_hi, m_lo, e_hi, e_lo, f_hi, f_lo, w_hi, w_lo, ids, columns,
    own, ritz, mats, inverses, panel, ids_sem, ritz_sem, mats_sem, panel_sem, sems, map_copy,
):
    node, core, side_of = place[1] * LOCAL, place[1] % 2, place[2]
    blocks, sep = own.shape[0] // BLK, panel.shape[0]
    per_core = blocks // 2
    parts = [(n, c) for n in range(LOCAL) for c in range(2)]
    copies = []
    for g in range(blocks):
        rows = pl.ds(g * BLK, BLK)
        copies.append(
            (
                pltpu.make_async_copy(inverses_hbm.at[:, :, g], inverses.at[g], sems.at[g, 0]),
                pltpu.make_async_copy(own_hbm.at[rows, :], own.at[rows, :], sems.at[g, 1]),
            )
        )
    my_mats = pltpu.make_async_copy(
        mats_hbm.at[pl.ds(side_of * per_core, per_core)], mats, mats_sem
    )
    whole_panel = pltpu.make_async_copy(panel_hbm.at[0], panel, panel_sem)
    small = [
        pltpu.make_async_copy(ritz_hbm, ritz, ritz_sem),
        pltpu.make_async_copy(sep_map, map_copy, ids_sem),
    ]
    for copy in [whole_panel, *copies[0], *sum(copies[1:], ()), my_mats] + small:
        copy.start()
    whole_panel.wait()
    for g in range(blocks):
        for copy in copies[g]:
            copy.wait()
        rows = slice(g * BLK, (g + 1) * BLK)
        own_hi[g], own_lo[g] = split(own[rows, :])
        weighted = []
        for n in range(LOCAL):
            weighted.append(inverses[g, n, 0] * constant(node + n, W_REAL))
            weighted.append(inverses[g, n, 1] * -constant(node + n, W_IMAG))
        w_hi[g], w_lo[g] = split(sum(weighted[1:], weighted[0]))
        p_hi, p_lo = split(panel[:, rows])
        d_hi, d_lo = split(jnp.concatenate([inverses[g, n, c] for n, c in parts], 1))
        e = dot(
            jnp.concatenate([p_hi, p_lo, p_hi], 1), jnp.concatenate([d_hi, d_hi, d_lo], 0)
        )
        d_hi, d_lo = split(
            jnp.concatenate([-inverses[g, n, c] if c == 0 else inverses[g, n, c] for n, c in parts], 0)
        )
        f = dot(
            jnp.concatenate([d_hi, d_lo, d_hi], 1),
            jnp.concatenate([p_hi, p_hi, p_lo], 1),
            ((1,), (1,)),
        )
        side, nth = divmod(g, per_core)
        cols = slice(nth * BLK, (nth + 1) * BLK)
        for k in range(2 * LOCAL):
            span, block = slice(k * sep, (k + 1) * sep), slice(k * BLK, (k + 1) * BLK)
            e_hi[side, span, cols], e_lo[side, span, cols] = split(e[:, block])
            f_hi[rows, span], f_lo[rows, span] = split(f[block, :])
    for copy in small:
        copy.wait()
    my_mats.wait()
    first, mid, quarter = place[1] // 2 == 0, own.shape[1] // 2, own.shape[0] // 4
    for side in range(2):
        top, bottom = (
            jnp.where(first, own[rows, :mid], own[rows, mid:])
            for rows in (slice(k * quarter, (k + 1) * quarter) for k in (2 * side, 2 * side + 1))
        )
        low, high = halves(top, bottom)
        columns[side] = jnp.where(core == 0, low, high)
    for g in range(per_core):
        rows = pl.ds(pl.multiple_of((side_of * per_core + g) * BLK, BLK), BLK)
        scaled[g] = own[rows, :] * ritz[...]
        m_hi[g], m_lo[g] = split(jnp.concatenate([mats[g, q] for q in range(4)], 1))
    lane = lax.broadcasted_iota(jnp.int32, ids.shape, 1)
    value = jnp.zeros(ids.shape, jnp.int32)
    for p in range(4):
        value = jnp.where(lane == p, map_copy[0, p], value)
    ids[...] = value.astype(F32)


def residual_kernel(
    place, lists, halo, own_hi, own_lo, scaled, m_hi, m_lo, residual, r_hi, r_lo, ext_hi, ext_lo
):
    sub, side = place[0], place[2]
    blocks, per_core = own_hi.shape[0], m_hi.shape[0]
    hi, lo = split(halo[...].reshape(HALO, BLK, halo.shape[1]))
    ext_hi[pl.ds(side * blocks, HALO)] = hi
    ext_lo[pl.ds(side * blocks, HALO)] = lo
    start = HALO - side * HALO
    ext_hi[pl.ds(start, blocks)] = own_hi[...]
    ext_lo[pl.ds(start, blocks)] = own_lo[...]
    for g in range(per_core):
        where = [lists[q, side * per_core + g] - sub * blocks + start for q in range(4)]
        rhs = [jnp.concatenate([e[w] for w in where], 0) for e in (ext_hi, ext_lo)]
        rows = slice(g * BLK, (g + 1) * BLK)
        res = dot3((m_hi[g], m_lo[g]), rhs) - scaled[g]
        residual[rows, :] = res
        r_hi[rows, :], r_lo[rows, :] = split(res)


def mine_kernel(place, e_hi, e_lo, r_hi, r_lo, sums):
    side = place[2]
    sums[...] = dot3((e_hi[side], e_lo[side]), (r_hi[...], r_lo[...]))


def theirs_kernel(
    place, sums, theirs, e_hi, e_lo, m_hi, m_lo, ids, r_hi, r_lo, pieces
):
    side = place[2]
    other = 1 - side
    hi, lo = split(theirs[...])
    r_hi[other], r_lo[other] = hi, lo
    r_hi[side], r_lo[side] = m_hi[...], m_lo[...]
    sep = e_hi.shape[1] // (2 * LOCAL)
    for k in range(2 * LOCAL):
        span = slice(k * sep, (k + 1) * sep)
        part = sums[span, :] + dot3((e_hi[other, span, :], e_lo[other, span, :]), (hi, lo))
        n, c = divmod(k, 2)
        for p in range(4):
            for h in range(2):
                row = ((p * 2 + c) * 2 + h) * 8
                tile = part[p * BLK : (p + 1) * BLK, h * LANES : (h + 1) * LANES]
                pieces[n * 16 : (n + 1) * 16, row : row + 8, :] = tile.reshape(16, 8, LANES)
    pieces[:, 128:136, :] = jnp.broadcast_to(ids[...][None], (32, 8, LANES))


def owner_kernel(place, maps, shift, received, back, total):
    sub = place[0]
    node = place[1] * LOCAL + sub // 16
    first_row = (sub % 16) * 8
    z_r, z_i, w_r, w_i = (constant(node, v) for v in (Z_REAL, Z_IMAG, W_REAL, W_IMAG))
    total[...] = jnp.zeros_like(total)

    def add(t, carry):
        groups = [maps[t, p] for p in range(4)]
        sums = [total[g] + received[t, p * 32 : (p + 1) * 32, :] for p, g in enumerate(groups)]
        for g, value in zip(groups, sums):
            total[g] = value
        return carry

    lax.fori_loop(0, 32, add, 0, unroll=4)
    lane = lax.broadcasted_iota(jnp.int32, (8, LANES), 1)
    pick = lane == first_row + lax.broadcasted_iota(jnp.int32, (8, LANES), 0)
    for g in range(GROUPS):
        row = jnp.broadcast_to(shift[g : g + 1, :], (8, LANES))
        gap = z_r - jnp.sum(jnp.where(pick, row, 0.0), axis=1, keepdims=True)
        gap = jnp.concatenate([gap, gap], 0)
        modulus = gap * gap + z_i * z_i
        real, imag = total[g, :16], total[g, 16:]
        c_r = (real * gap + imag * z_i) / modulus
        c_i = (imag * gap - real * z_i) / modulus
        total[g, :16] = w_r * c_r - w_i * c_i
        total[g, 16:] = w_r * c_i + w_i * c_r

    def give(t, carry):
        for p in range(4):
            back[t, p * 32 : (p + 1) * 32, :] = total[maps[t, p]]
        return carry

    lax.fori_loop(0, 32, give, 0, unroll=4)


def coarse_halves(picked, x_hi, x_lo):
    sep = x_hi.shape[0] // (2 * LOCAL)
    for k in range(2 * LOCAL):
        n, c = divmod(k, 2)
        for p in range(4):
            for h in range(2):
                row = ((p * 2 + c) * 2 + h) * 8
                tile = picked[n * 16 : (n + 1) * 16, row : row + 8, :].reshape(BLK, LANES)
                rows = slice(k * sep + p * BLK, k * sep + (p + 1) * BLK)
                cols = slice(h * LANES, (h + 1) * LANES)
                x_hi[rows, cols], x_lo[rows, cols] = split(tile)


def solve(side, core, coarse, f_hi, f_lo, r_hi, r_lo, w_hi, w_lo, keep, send):
    per_side = w_hi.shape[0] // 2
    quarters = []
    for g in range(0, per_side, 2):
        first = side * per_side + g
        both = slice(first * BLK, (first + 2) * BLK)
        back = dot3((f_hi[both, :], f_lo[both, :]), coarse)
        local = []
        for i in range(2):
            rows = slice((g + i) * BLK, (g + i + 1) * BLK)
            local.append(
                dot3((w_hi[first + i], w_lo[first + i]), (r_hi[side, rows, :], r_lo[side, rows, :]))
            )
        quarters.append(back + jnp.concatenate(local, 0))
    for chip in range(2):
        cols = slice(chip * LANES, (chip + 1) * LANES)
        low, high = halves(quarters[0][:, cols], quarters[1][:, cols])
        keep[chip] = jnp.where(core == 0, low, high)
        send[chip] = jnp.where(core == 0, high, low)


def first_kernel(place, picked, f_hi, f_lo, r_hi, r_lo, w_hi, w_lo, keep, send, x_hi, x_lo):
    coarse_halves(picked, x_hi, x_lo)
    coarse = x_hi[...], x_lo[...]
    solve(0, place[1] % 2, coarse, f_hi, f_lo, r_hi, r_lo, w_hi, w_lo, keep, send)


def second_kernel(place, x_hi, x_lo, f_hi, f_lo, r_hi, r_lo, w_hi, w_lo, keep, send):
    coarse = x_hi[...], x_lo[...]
    solve(1, place[1] % 2, coarse, f_hi, f_lo, r_hi, r_lo, w_hi, w_lo, keep, send)


def scale_kernel(rows, update_a, update_b, squares, out):
    quarter = update_a.shape[0]
    factor = lax.rsqrt(jnp.sum(squares[...], axis=0) / rows + 1e-06)
    for side, update in enumerate((update_a, update_b)):
        new = (update[...] * factor).T
        for h in range(2):
            start = (2 * side + h) * quarter
            out[:, start : start + quarter] = new[h * (LANES // 2) : (h + 1) * (LANES // 2)]


def call(body, name, specs, shapes, scratch=(), limit=16, flops=0):
    shapes = [s if isinstance(s, jax.ShapeDtypeStruct) else jax.ShapeDtypeStruct(s, F32) for s in shapes]
    return pl.pallas_call(
        body,
        name=name,
        in_specs=specs,
        out_specs=[VMEM] * len(shapes),
        out_shape=shapes,
        scratch_shapes=list(scratch),
        cost_estimate=pl.CostEstimate(flops=flops, bytes_accessed=8 << 20, transcendentals=0),
        compiler_params=pltpu.CompilerParams(vmem_limit_bytes=limit << 20),
    )


def shards(
    search_vectors,
    ritz_values,
    matrix_blocks,
    block_lists,
    inverses,
    panels,
    separator_map,
    separator_shift,
):
    rows, width = search_vectors.shape
    subs, nodes = lax.axis_size("sub"), lax.axis_size("node")
    sub, node = lax.axis_index("sub"), lax.axis_index("node")
    side = (node + sub) % 2
    place = jnp.stack([sub, node, side]).astype(jnp.int32)

    halo_rows = HALO * BLK
    edge = lax.dynamic_slice_in_dim(
        search_vectors, jnp.where(side == 1, rows - halo_rows, 0), halo_rows, 0
    )
    ring = []
    for t in range(subs):
        for n in range(nodes):
            d = t + 1 if (n + t) % 2 == 1 else t - 1
            if 0 <= d < subs:
                ring.append((t * nodes + n, d * nodes + (n ^ 2)))
    swap_core = [(i, i ^ 1) for i in range(nodes)]
    swap_chip = [(i, i ^ 2) for i in range(nodes)]
    halo = lax.ppermute(edge, ("sub", "node"), ring)

    half = functools.partial(jax.ShapeDtypeStruct, dtype=BF16)
    blocks, sep = rows // BLK, panels.shape[1]
    per_core = blocks // 2
    prepared = call(
        prepare_kernel,
        "prepare",
        [SMEM] + [HBM] * 6,
        [half((blocks, BLK, width))] * 2
        + [(per_core, BLK, width)]
        + [half((per_core, BLK, 4 * BLK))] * 2
        + [half((2, 4 * sep, rows // 2))] * 2
        + [half((rows, 4 * sep))] * 2
        + [half((blocks, BLK, BLK))] * 2
        + [(8, LANES), (2, rows // 4, LANES)],
        [
            pltpu.VMEM((rows, width), F32),
            pltpu.VMEM((1, width), F32),
            pltpu.VMEM((per_core, 4, BLK, BLK), F32),
            pltpu.VMEM((blocks, LOCAL, 2, BLK, BLK), F32),
            pltpu.VMEM((sep, rows), F32),
            pltpu.SemaphoreType.DMA,
            pltpu.SemaphoreType.DMA,
            pltpu.SemaphoreType.DMA,
            pltpu.SemaphoreType.DMA,
            pltpu.SemaphoreType.DMA((blocks, 2)),
            pltpu.SMEM(separator_map.shape, jnp.int32),
        ],
        limit=24,
        flops=8 * 10**9,
    )(
        place, *(
            pltpu.with_memory_space_constraint(x, pltpu.HBM)
            for x in (
                separator_map, search_vectors, ritz_values[None, :],
                matrix_blocks, inverses, panels,
            )
        )
    )
    own_hi, own_lo, scaled, m_hi, m_lo, e_hi, e_lo, f_hi, f_lo, w_hi, w_lo, ids, columns = prepared
    halo, ids = lax.optimization_barrier((halo, ids))
    residual, mine_hi, mine_lo = call(
        residual_kernel,
        "residual",
        [SMEM, SMEM] + [VMEM] * 6,
        [(rows // 2, width)] + [half((rows // 2, width))] * 2,
        [pltpu.VMEM((blocks + HALO, BLK, width), BF16)] * 2,
        flops=10**9,
    )(place, block_lists.T, halo, own_hi, own_lo, scaled, m_hi, m_lo)
    theirs = lax.ppermute(residual, "node", swap_core)
    (sums,) = call(
        mine_kernel,
        "mine",
        [SMEM] + [VMEM] * 4,
        [(4 * sep, width)],
        flops=4 * 10**9,
    )(place, e_hi, e_lo, mine_hi, mine_lo)
    theirs, sums = lax.optimization_barrier((theirs, sums))
    r_hi, r_lo, pieces = call(
        theirs_kernel,
        "theirs",
        [SMEM] + [VMEM] * 7,
        [half((2, rows // 2, width))] * 2 + [(subs, 136, LANES)],
        flops=4 * 10**9,
    )(place, sums, theirs, e_hi, e_lo, mine_hi, mine_lo, ids)
    received = lax.all_to_all(pieces, "sub", 0, 0, tiled=True)
    maps = received[:, 128, :4].astype(jnp.int32)
    (back,) = call(
        owner_kernel,
        "owner",
        [SMEM, SMEM, VMEM, VMEM],
        [(subs, 128, LANES)],
        [pltpu.VMEM((GROUPS, 32, LANES), F32)],
    )(place, maps, separator_shift.reshape(GROUPS, LANES), received)
    picked = lax.all_to_all(back, "sub", 0, 0, tiled=True)
    operators = (f_hi, f_lo, r_hi, r_lo, w_hi, w_lo)
    keep_a, send_a, x_hi, x_lo = call(
        first_kernel,
        "first",
        [SMEM] + [VMEM] * 7,
        [(2, rows // 4, LANES)] * 2 + [half((4 * sep, width))] * 2,
        flops=2 * 10**9,
    )(place, picked, *operators)
    theirs_a = lax.ppermute(send_a, "node", swap_core)
    keep_b, send_b = call(
        second_kernel,
        "second",
        [SMEM] + [VMEM] * 8,
        [(2, rows // 4, LANES)] * 2,
        flops=2 * 10**9,
    )(place, x_hi, x_lo, *operators)
    theirs_a, send_b = lax.optimization_barrier((theirs_a, send_b))
    theirs_b = lax.ppermute(send_b, "node", swap_core)
    chip = node // 2

    def both(index, keep, theirs):
        return lax.dynamic_index_in_dim(keep, index, 0, False) + lax.dynamic_index_in_dim(
            theirs, index, 0, False
        )

    far_a = lax.ppermute(both(1 - chip, keep_a, theirs_a), "node", swap_chip)
    far_b = lax.ppermute(both(1 - chip, keep_b, theirs_b), "node", swap_chip)
    update_a = columns[0] - (both(chip, keep_a, theirs_a) + far_a)
    update_b = columns[1] - (both(chip, keep_b, theirs_b) + far_b)
    sums = jnp.sum(update_a * update_a, axis=0) + jnp.sum(update_b * update_b, axis=0)
    sums = sums + jnp.roll(sums, LANES // 2)
    squares = jnp.broadcast_to(sums[None, None], (subs, 1, LANES))
    gathered = lax.all_to_all(squares, "sub", 0, 0, tiled=True)
    (out,) = call(
        functools.partial(scale_kernel, rows * subs),
        "scale",
        [VMEM, VMEM, VMEM],
        [(width // nodes, rows)],
    )(update_a, update_b, gathered)
    return out.T


def solution(mesh):
    return jax.shard_map(
        shards,
        mesh=mesh,
        in_specs=(
            P("sub", None),
            P(),
            P("sub", None, None, None),
            P("sub", None),
            P("node", None, "sub", None, None),
            P("sub", None, None),
            P("sub", None),
            P(),
        ),
        out_specs=P("sub", "node"),
        check_vma=False,
    )
```

```python
import functools
import math

import jax
import jax.numpy as jnp
from jax import lax
from jax.experimental import pallas as pl
from jax.experimental.pallas import tpu as pltpu
from jax.sharding import PartitionSpec as P

BLK = 128
HALO = 4
GROUPS = 8
NODES = 8
LOCAL = 2
LANES = 128

F32 = jnp.float32
BF16 = jnp.bfloat16
VMEM = pl.BlockSpec(memory_space=pltpu.VMEM)
SMEM = pl.BlockSpec(memory_space=pltpu.SMEM)
HBM = pl.BlockSpec(memory_space=pltpu.HBM)

THETA = [math.pi * (j + 0.5) / NODES for j in range(NODES)]
Z_REAL, Z_IMAG = [math.cos(t) for t in THETA], [math.sin(t) for t in THETA]
W_REAL, W_IMAG = [2.0 * v / NODES for v in Z_REAL], [2.0 * v / NODES for v in Z_IMAG]


def split(x):
    hi = x.astype(BF16)
    return hi, (x - hi.astype(F32)).astype(BF16)


def dot(a, b, dims=((1,), (0,))):
    return lax.dot_general(a, b, (dims, ((), ())), preferred_element_type=F32)


def dot3(a, b, dims=((1,), (0,))):
    return dot(a[0], b[0], dims) + (dot(a[0], b[1], dims) + dot(a[1], b[0], dims))


def halves(top, bottom):
    low = lax.broadcasted_iota(jnp.int32, top.shape, 1) < LANES // 2
    return (
        jnp.where(low, top, pltpu.roll(bottom, LANES // 2, 1)),
        jnp.where(low, pltpu.roll(top, LANES // 2, 1), bottom),
    )


def constant(node, values):
    out = jnp.float32(values[0])
    for k in range(1, NODES):
        out = jnp.where(node == k, jnp.float32(values[k]), out)
    return out


def prepare_kernel(
    place, sep_map, own_hbm, ritz_hbm, mats_hbm, inverses_hbm, panel_hbm,
    own_hi, own_lo, scaled, m_hi, m_lo, e_hi, e_lo, f_hi, f_lo, w_hi, w_lo, ids, columns,
    own, ritz, mats, inverses, panel, ids_sem, ritz_sem, mats_sem, panel_sem, sems, map_copy,
):
    node, core, side_of = place[1] * LOCAL, place[1] % 2, place[2]
    blocks, sep = own.shape[0] // BLK, panel.shape[0]
    per_core = blocks // 2
    parts = [(n, c) for n in range(LOCAL) for c in range(2)]
    copies = []
    for g in range(blocks):
        rows = pl.ds(g * BLK, BLK)
        copies.append(
            (
                pltpu.make_async_copy(inverses_hbm.at[:, :, g], inverses.at[g], sems.at[g, 0]),
                pltpu.make_async_copy(own_hbm.at[rows, :], own.at[rows, :], sems.at[g, 1]),
            )
        )
    my_mats = pltpu.make_async_copy(
        mats_hbm.at[pl.ds(side_of * per_core, per_core)], mats, mats_sem
    )
    whole_panel = pltpu.make_async_copy(panel_hbm.at[0], panel, panel_sem)
    small = [
        pltpu.make_async_copy(ritz_hbm, ritz, ritz_sem),
        pltpu.make_async_copy(sep_map, map_copy, ids_sem),
    ]
    for copy in [whole_panel, *copies[0], *sum(copies[1:], ()), my_mats] + small:
        copy.start()
    whole_panel.wait()
    for g in range(blocks):
        for copy in copies[g]:
            copy.wait()
        rows = slice(g * BLK, (g + 1) * BLK)
        own_hi[g], own_lo[g] = split(own[rows, :])
        weighted = []
        for n in range(LOCAL):
            weighted.append(inverses[g, n, 0] * constant(node + n, W_REAL))
            weighted.append(inverses[g, n, 1] * -constant(node + n, W_IMAG))
        w_hi[g], w_lo[g] = split(sum(weighted[1:], weighted[0]))
        p_hi, p_lo = split(panel[:, rows])
        d_hi, d_lo = split(jnp.concatenate([inverses[g, n, c] for n, c in parts], 1))
        e = dot(
            jnp.concatenate([p_hi, p_lo, p_hi], 1), jnp.concatenate([d_hi, d_hi, d_lo], 0)
        )
        d_hi, d_lo = split(
            jnp.concatenate([-inverses[g, n, c] if c == 0 else inverses[g, n, c] for n, c in parts], 0)
        )
        f = dot(
            jnp.concatenate([d_hi, d_lo, d_hi], 1),
            jnp.concatenate([p_hi, p_hi, p_lo], 1),
            ((1,), (1,)),
        )
        side, nth = divmod(g, per_core)
        cols = slice(nth * BLK, (nth + 1) * BLK)
        for k in range(2 * LOCAL):
            span, block = slice(k * sep, (k + 1) * sep), slice(k * BLK, (k + 1) * BLK)
            e_hi[side, span, cols], e_lo[side, span, cols] = split(e[:, block])
            f_hi[rows, span], f_lo[rows, span] = split(f[block, :])
    for copy in small:
        copy.wait()
    my_mats.wait()
    first, mid, quarter = place[1] // 2 == 0, own.shape[1] // 2, own.shape[0] // 4
    for side in range(2):
        top, bottom = (
            jnp.where(first, own[rows, :mid], own[rows, mid:])
            for rows in (slice(k * quarter, (k + 1) * quarter) for k in (2 * side, 2 * side + 1))
        )
        low, high = halves(top, bottom)
        columns[side] = jnp.where(core == 0, low, high)
    for g in range(per_core):
        rows = pl.ds(pl.multiple_of((side_of * per_core + g) * BLK, BLK), BLK)
        scaled[g] = own[rows, :] * ritz[...]
        m_hi[g], m_lo[g] = split(jnp.concatenate([mats[g, q] for q in range(4)], 1))
    lane = lax.broadcasted_iota(jnp.int32, ids.shape, 1)
    value = jnp.zeros(ids.shape, jnp.int32)
    for p in range(4):
        value = jnp.where(lane == p, map_copy[0, p], value)
    ids[...] = value.astype(F32)


def residual_kernel(
    place, lists, halo, own_hi, own_lo, scaled, m_hi, m_lo, residual, r_hi, r_lo, ext_hi, ext_lo
):
    sub, side = place[0], place[2]
    blocks, per_core = own_hi.shape[0], m_hi.shape[0]
    hi, lo = split(halo[...].reshape(HALO, BLK, halo.shape[1]))
    ext_hi[pl.ds(side * blocks, HALO)] = hi
    ext_lo[pl.ds(side * blocks, HALO)] = lo
    start = HALO - side * HALO
    ext_hi[pl.ds(start, blocks)] = own_hi[...]
    ext_lo[pl.ds(start, blocks)] = own_lo[...]
    for g in range(per_core):
        where = [lists[q, side * per_core + g] - sub * blocks + start for q in range(4)]
        rhs = [jnp.concatenate([e[w] for w in where], 0) for e in (ext_hi, ext_lo)]
        rows = slice(g * BLK, (g + 1) * BLK)
        res = dot3((m_hi[g], m_lo[g]), rhs) - scaled[g]
        residual[rows, :] = res
        r_hi[rows, :], r_lo[rows, :] = split(res)


def mine_kernel(place, e_hi, e_lo, r_hi, r_lo, sums):
    side = place[2]
    sums[...] = dot3((e_hi[side], e_lo[side]), (r_hi[...], r_lo[...]))


def theirs_kernel(
    place, sums, theirs, e_hi, e_lo, m_hi, m_lo, ids, r_hi, r_lo, pieces
):
    side = place[2]
    other = 1 - side
    hi, lo = split(theirs[...])
    r_hi[other], r_lo[other] = hi, lo
    r_hi[side], r_lo[side] = m_hi[...], m_lo[...]
    sep = e_hi.shape[1] // (2 * LOCAL)
    for k in range(2 * LOCAL):
        span = slice(k * sep, (k + 1) * sep)
        part = sums[span, :] + dot3((e_hi[other, span, :], e_lo[other, span, :]), (hi, lo))
        n, c = divmod(k, 2)
        for p in range(4):
            for h in range(2):
                row = ((p * 2 + c) * 2 + h) * 8
                tile = part[p * BLK : (p + 1) * BLK, h * LANES : (h + 1) * LANES]
                pieces[n * 16 : (n + 1) * 16, row : row + 8, :] = tile.reshape(16, 8, LANES)
    pieces[:, 128:136, :] = jnp.broadcast_to(ids[...][None], (32, 8, LANES))


def owner_kernel(place, maps, shift, received, back, total):
    sub = place[0]
    node = place[1] * LOCAL + sub // 16
    first_row = (sub % 16) * 8
    z_r, z_i, w_r, w_i = (constant(node, v) for v in (Z_REAL, Z_IMAG, W_REAL, W_IMAG))
    total[...] = jnp.zeros_like(total)

    def add(t, carry):
        groups = [maps[t, p] for p in range(4)]
        sums = [total[g] + received[t, p * 32 : (p + 1) * 32, :] for p, g in enumerate(groups)]
        for g, value in zip(groups, sums):
            total[g] = value
        return carry

    lax.fori_loop(0, 32, add, 0, unroll=4)
    lane = lax.broadcasted_iota(jnp.int32, (8, LANES), 1)
    pick = lane == first_row + lax.broadcasted_iota(jnp.int32, (8, LANES), 0)
    for g in range(GROUPS):
        row = jnp.broadcast_to(shift[g : g + 1, :], (8, LANES))
        gap = z_r - jnp.sum(jnp.where(pick, row, 0.0), axis=1, keepdims=True)
        gap = jnp.concatenate([gap, gap], 0)
        modulus = gap * gap + z_i * z_i
        real, imag = total[g, :16], total[g, 16:]
        c_r = (real * gap + imag * z_i) / modulus
        c_i = (imag * gap - real * z_i) / modulus
        total[g, :16] = w_r * c_r - w_i * c_i
        total[g, 16:] = w_r * c_i + w_i * c_r

    def give(t, carry):
        for p in range(4):
            back[t, p * 32 : (p + 1) * 32, :] = total[maps[t, p]]
        return carry

    lax.fori_loop(0, 32, give, 0, unroll=4)


def coarse_halves(picked, x_hi, x_lo):
    sep = x_hi.shape[0] // (2 * LOCAL)
    for k in range(2 * LOCAL):
        n, c = divmod(k, 2)
        for p in range(4):
            for h in range(2):
                row = ((p * 2 + c) * 2 + h) * 8
                tile = picked[n * 16 : (n + 1) * 16, row : row + 8, :].reshape(BLK, LANES)
                rows = slice(k * sep + p * BLK, k * sep + (p + 1) * BLK)
                cols = slice(h * LANES, (h + 1) * LANES)
                x_hi[rows, cols], x_lo[rows, cols] = split(tile)


def solve(side, core, coarse, f_hi, f_lo, r_hi, r_lo, w_hi, w_lo, keep, send):
    per_side = w_hi.shape[0] // 2
    quarters = []
    for g in range(0, per_side, 2):
        first = side * per_side + g
        both = slice(first * BLK, (first + 2) * BLK)
        back = dot3((f_hi[both, :], f_lo[both, :]), coarse)
        local = []
        for i in range(2):
            rows = slice((g + i) * BLK, (g + i + 1) * BLK)
            local.append(
                dot3((w_hi[first + i], w_lo[first + i]), (r_hi[side, rows, :], r_lo[side, rows, :]))
            )
        quarters.append(back + jnp.concatenate(local, 0))
    for chip in range(2):
        cols = slice(chip * LANES, (chip + 1) * LANES)
        low, high = halves(quarters[0][:, cols], quarters[1][:, cols])
        keep[chip] = jnp.where(core == 0, low, high)
        send[chip] = jnp.where(core == 0, high, low)


def first_kernel(place, picked, f_hi, f_lo, r_hi, r_lo, w_hi, w_lo, keep, send, x_hi, x_lo):
    coarse_halves(picked, x_hi, x_lo)
    coarse = x_hi[...], x_lo[...]
    solve(0, place[1] % 2, coarse, f_hi, f_lo, r_hi, r_lo, w_hi, w_lo, keep, send)


def second_kernel(place, x_hi, x_lo, f_hi, f_lo, r_hi, r_lo, w_hi, w_lo, keep, send):
    coarse = x_hi[...], x_lo[...]
    solve(1, place[1] % 2, coarse, f_hi, f_lo, r_hi, r_lo, w_hi, w_lo, keep, send)


def scale_kernel(rows, update_a, update_b, squares, out):
    quarter = update_a.shape[0]
    factor = lax.rsqrt(jnp.sum(squares[...], axis=0) / rows + 1e-06)
    for side, update in enumerate((update_a, update_b)):
        new = (update[...] * factor).T
        for h in range(2):
            start = (2 * side + h) * quarter
            out[:, start : start + quarter] = new[h * (LANES // 2) : (h + 1) * (LANES // 2)]


def call(body, name, specs, shapes, scratch=(), limit=16, flops=0):
    shapes = [s if isinstance(s, jax.ShapeDtypeStruct) else jax.ShapeDtypeStruct(s, F32) for s in shapes]
    return pl.pallas_call(
        body,
        name=name,
        in_specs=specs,
        out_specs=[VMEM] * len(shapes),
        out_shape=shapes,
        scratch_shapes=list(scratch),
        cost_estimate=pl.CostEstimate(flops=flops, bytes_accessed=8 << 20, transcendentals=0),
        compiler_params=pltpu.CompilerParams(vmem_limit_bytes=limit << 20),
    )


def shards(
    search_vectors,
    ritz_values,
    matrix_blocks,
    block_lists,
    inverses,
    panels,
    separator_map,
    separator_shift,
):
    rows, width = search_vectors.shape
    subs, nodes = lax.axis_size("sub"), lax.axis_size("node")
    sub, node = lax.axis_index("sub"), lax.axis_index("node")
    side = (node + sub + 1) % 2
    place = jnp.stack([sub, node, side]).astype(jnp.int32)

    halo_rows = HALO * BLK
    edge = lax.dynamic_slice_in_dim(
        search_vectors, jnp.where(side == 1, rows - halo_rows, 0), halo_rows, 0
    )
    ring = []
    for t in range(subs):
        for n in range(nodes):
            d = t + 1 if (n + t) % 2 == 0 else t - 1
            if 0 <= d < subs:
                ring.append((t * nodes + n, d * nodes + (n ^ 2)))
    swap_core = [(i, i ^ 1) for i in range(nodes)]
    swap_chip = [(i, i ^ 2) for i in range(nodes)]
    halo = lax.ppermute(edge, ("sub", "node"), ring)

    half = functools.partial(jax.ShapeDtypeStruct, dtype=BF16)
    blocks, sep = rows // BLK, panels.shape[1]
    per_core = blocks // 2
    prepared = call(
        prepare_kernel,
        "prepare",
        [SMEM] + [HBM] * 6,
        [half((blocks, BLK, width))] * 2
        + [(per_core, BLK, width)]
        + [half((per_core, BLK, 4 * BLK))] * 2
        + [half((2, 4 * sep, rows // 2))] * 2
        + [half((rows, 4 * sep))] * 2
        + [half((blocks, BLK, BLK))] * 2
        + [(8, LANES), (2, rows // 4, LANES)],
        [
            pltpu.VMEM((rows, width), F32),
            pltpu.VMEM((1, width), F32),
            pltpu.VMEM((per_core, 4, BLK, BLK), F32),
            pltpu.VMEM((blocks, LOCAL, 2, BLK, BLK), F32),
            pltpu.VMEM((sep, rows), F32),
            pltpu.SemaphoreType.DMA,
            pltpu.SemaphoreType.DMA,
            pltpu.SemaphoreType.DMA,
            pltpu.SemaphoreType.DMA,
            pltpu.SemaphoreType.DMA((blocks, 2)),
            pltpu.SMEM(separator_map.shape, jnp.int32),
        ],
        limit=24,
        flops=8 * 10**9,
    )(
        place, *(
            pltpu.with_memory_space_constraint(x, pltpu.HBM)
            for x in (
                separator_map, search_vectors, ritz_values[None, :],
                matrix_blocks, inverses, panels,
            )
        )
    )
    own_hi, own_lo, scaled, m_hi, m_lo, e_hi, e_lo, f_hi, f_lo, w_hi, w_lo, ids, columns = prepared
    halo, ids = lax.optimization_barrier((halo, ids))
    residual, mine_hi, mine_lo = call(
        residual_kernel,
        "residual",
        [SMEM, SMEM] + [VMEM] * 6,
        [(rows // 2, width)] + [half((rows // 2, width))] * 2,
        [pltpu.VMEM((blocks + HALO, BLK, width), BF16)] * 2,
        flops=10**9,
    )(place, block_lists.T, halo, own_hi, own_lo, scaled, m_hi, m_lo)
    theirs = lax.ppermute(residual, "node", swap_core)
    (sums,) = call(
        mine_kernel,
        "mine",
        [SMEM] + [VMEM] * 4,
        [(4 * sep, width)],
        flops=4 * 10**9,
    )(place, e_hi, e_lo, mine_hi, mine_lo)
    theirs, sums = lax.optimization_barrier((theirs, sums))
    r_hi, r_lo, pieces = call(
        theirs_kernel,
        "theirs",
        [SMEM] + [VMEM] * 7,
        [half((2, rows // 2, width))] * 2 + [(subs, 136, LANES)],
        flops=4 * 10**9,
    )(place, sums, theirs, e_hi, e_lo, mine_hi, mine_lo, ids)
    received = lax.all_to_all(pieces, "sub", 0, 0, tiled=True)
    maps = received[:, 128, :4].astype(jnp.int32)
    (back,) = call(
        owner_kernel,
        "owner",
        [SMEM, SMEM, VMEM, VMEM],
        [(subs, 128, LANES)],
        [pltpu.VMEM((GROUPS, 32, LANES), F32)],
    )(place, maps, separator_shift.reshape(GROUPS, LANES), received)
    picked = lax.all_to_all(back, "sub", 0, 0, tiled=True)
    operators = (f_hi, f_lo, r_hi, r_lo, w_hi, w_lo)
    keep_a, send_a, x_hi, x_lo = call(
        first_kernel,
        "first",
        [SMEM] + [VMEM] * 7,
        [(2, rows // 4, LANES)] * 2 + [half((4 * sep, width))] * 2,
        flops=2 * 10**9,
    )(place, picked, *operators)
    theirs_a = lax.ppermute(send_a, "node", swap_core)
    keep_b, send_b = call(
        second_kernel,
        "second",
        [SMEM] + [VMEM] * 8,
        [(2, rows // 4, LANES)] * 2,
        flops=2 * 10**9,
    )(place, x_hi, x_lo, *operators)
    theirs_a, send_b = lax.optimization_barrier((theirs_a, send_b))
    theirs_b = lax.ppermute(send_b, "node", swap_core)
    chip = node // 2

    def both(index, keep, theirs):
        return lax.dynamic_index_in_dim(keep, index, 0, False) + lax.dynamic_index_in_dim(
            theirs, index, 0, False
        )

    far_a = lax.ppermute(both(1 - chip, keep_a, theirs_a), "node", swap_chip)
    far_b = lax.ppermute(both(1 - chip, keep_b, theirs_b), "node", swap_chip)
    update_a = columns[0] - (both(chip, keep_a, theirs_a) + far_a)
    update_b = columns[1] - (both(chip, keep_b, theirs_b) + far_b)
    sums = jnp.sum(update_a * update_a, axis=0) + jnp.sum(update_b * update_b, axis=0)
    sums = sums + jnp.roll(sums, LANES // 2)
    squares = jnp.broadcast_to(sums[None, None], (subs, 1, LANES))
    gathered = lax.all_to_all(squares, "sub", 0, 0, tiled=True)
    (out,) = call(
        functools.partial(scale_kernel, rows * subs),
        "scale",
        [VMEM, VMEM, VMEM],
        [(width // nodes, rows)],
    )(update_a, update_b, gathered)
    return out.T


def solution(mesh):
    return jax.shard_map(
        shards,
        mesh=mesh,
        in_specs=(
            P("sub", None),
            P(),
            P("sub", None, None, None),
            P("sub", None),
            P("node", None, "sub", None, None),
            P("sub", None, None),
            P("sub", None),
            P(),
        ),
        out_specs=P("sub", "node"),
        check_vma=False,
    )
```
